32 devices in a mesh: fsdp: 8 (over z, core), solve: 4 (over y, x).
Axes of the slice: x: 2, y: 2, z: 4, core: 2. Of those that a mesh axis runs over, the one named last changes fastest.
Arguments:
- inputs: bfloat16 [6144, 8192], P('fsdp', 'solve'), may hold values from -6 to 6
- cotangent: bfloat16 [6144, 8192], P('fsdp', 'solve'), may hold values from -6 to 6
- gate_pre: bfloat16 [6144, 14336], P('fsdp', 'solve'), may hold values from -6 to 6
- up_pre: bfloat16 [6144, 14336], P('fsdp', 'solve'), may hold values from -6 to 6
- down_weight: bfloat16 [14336, 8192], P('solve', 'fsdp'), may hold values from -0.046875 to 0.046875
- proj_model: bfloat16 [8192, 128], P('solve'), may hold values from -0.0625 to 0.0625
- proj_hidden: bfloat16 [14336, 128], P('solve'), may hold values from -0.046875 to 0.046875
- lengths: int32 [24], P('fsdp'), may hold values from 64 to 256
- gram: float32 [8192, 8192], P('fsdp', 'solve'), may hold values from -6 to 6
- inverse_factor: float32 [8192, 8192], P('fsdp', 'solve'), as said below
- queries: float32 [8192, 256], P('solve', 'fsdp'), may hold values from -6 to 6
Outputs:
- new_gram: float32 [8192, 8192], P('fsdp', 'solve')
- whitened: float32 [8192, 256], P(('fsdp', 'solve'))
- scores: float32 [24, 256], replicated
The draws below stay inside these ranges and needn't reach their ends.
Inputs may be any that keep to these rules, and one draw needn't show every extreme that they name: `inverse_factor`: zero above the diagonal; diagonal entries between 0.5 and 3.
All inputs are finite; a program needn't handle non-finite values.
Results may differ from the reference program's by a relative error of at most 0.0032.
Values may be sent and summed in bfloat16 or wider, within the bound.
No kernel may reach another device: no remote copies, remote signals or barrier semaphores. Data moves between devices by JAX's collectives and lax.ppermute only.
A program may use at most 192 MiB of HBM per device.

```python
import math
import jax
import jax.numpy as jnp
from jax import lax

D = 8192
FF = 14336
KP = 64
K = 8192
SEQ_LEN = 256
QUERIES = 256
EXAMPLES = 24
TOKENS = 6144


def draw_inverse_factor(key, part):
    first, second = jax.random.split(jax.random.fold_in(key, 11))
    spread = 0.5
    diagonal = jax.random.uniform(second, (K,), jnp.float32, 1.0, 2.0)
    off_part = jax.random.normal(first, (K, K), jnp.float32) * (spread / math.sqrt(K))
    return jnp.tril(off_part, -1) + jnp.diag(diagonal)


def with_ends(entries, rng, smallest, high):
    longest = entries.shape.index(max(entries.shape))
    spots = []
    for shift in (0, 1):
        where = [jax.random.randint(jax.random.fold_in(rng, axis), (), 0, length) for axis, length in enumerate(entries.shape)]
        where[longest] = (where[longest] + shift) % entries.shape[longest]
        spots.append(tuple(where))
    return entries.at[spots[0]].set(smallest).at[spots[1]].set(high)


def level_of(stream_key, shape, cuts, low, largest):
    def one(dim, blocks):
        heights = jax.random.uniform(jax.random.fold_in(jax.random.fold_in(stream_key, 6), dim), (blocks,), jnp.float32, low / len(cuts), largest / len(cuts))
        return jnp.repeat(jnp.exp(heights), shape[dim] // blocks).reshape((-1,) + (1,) * (len(shape) - dim - 1))

    level = one(*cuts[0])
    for cut in cuts[1:]:
        level = level * one(*cut)
    return level


def noise(key, dims, scale, reach, cuts=(), kind=jnp.bfloat16):
    array = scale * jax.random.normal(key, dims, jnp.float32)
    if cuts:
        array = array * level_of(key, dims, cuts, -0.22, 0.18)
    return jnp.clip(array, -reach, reach).astype(kind)


def setup_inputs(seed: int = 0) -> dict:
    key_list = jax.random.split(jax.random.key(seed), 12)
    return {
        "inputs": noise(key_list[0], (TOKENS, D), 1.0, 6.0, ((0, 8), (1, 4))),
        "cotangent": noise(key_list[1], (TOKENS, D), 1.0, 6.0, ((0, 8), (1, 4))),
        "gate_pre": noise(key_list[2], (TOKENS, FF), 1.0, 6.0, ((0, 8), (1, 4))),
        "up_pre": noise(key_list[3], (TOKENS, FF), 1.0, 6.0, ((0, 8), (1, 4))),
        "down_weight": noise(key_list[4], (FF, D), FF ** -0.5, 0.046875, ((0, 4), (1, 8))),
        "proj_model": noise(key_list[5], (D, 2 * KP), D ** -0.5, 0.0625, ((0, 4),)),
        "proj_hidden": noise(key_list[6], (FF, 2 * KP), FF ** -0.5, 0.046875, ((0, 4),)),
        "lengths": with_ends(jax.random.randint(key_list[7], (EXAMPLES,), SEQ_LEN // 4, SEQ_LEN + 1), jax.random.fold_in(key_list[7], 1), SEQ_LEN // 4, SEQ_LEN).astype(jnp.int32),
        "gram": noise(key_list[8], (K, K), 1.0, 6.0, ((0, 8), (1, 4)), jnp.float32),
        "inverse_factor": draw_inverse_factor(jax.random.fold_in(key_list[11], 71), 0),
        "queries": noise(key_list[10], (K, QUERIES), 1.0, 6.0, ((0, 4), (1, 8)), jnp.float32),
    }


def reference(inputs, cotangent, gate_pre, up_pre, down_weight, proj_model, proj_hidden, lengths, gram, inverse_factor, queries):
    top = lax.Precision.HIGHEST
    token_index = jnp.arange(TOKENS, dtype=jnp.int32)
    position = token_index % SEQ_LEN
    sequence = token_index // SEQ_LEN
    live = position < lengths[sequence]
    masked = jnp.where(live[:, None], cotangent, jnp.zeros_like(cotangent))
    grad_hidden = jnp.dot(masked, down_weight.T, preferred_element_type=jnp.float32)
    gate = gate_pre.astype(jnp.float32)
    smooth = gate * jax.nn.sigmoid(gate)
    hidden = (smooth * up_pre.astype(jnp.float32)).astype(jnp.bfloat16)
    grad_up = (grad_hidden * smooth).astype(jnp.bfloat16)
    out_down = jnp.dot(masked, proj_model[:, :KP], preferred_element_type=jnp.float32)
    in_up = jnp.dot(inputs, proj_model[:, KP:], preferred_element_type=jnp.float32)
    in_down = jnp.dot(hidden, proj_hidden[:, :KP], preferred_element_type=jnp.float32)
    out_up = jnp.dot(grad_up, proj_hidden[:, KP:], preferred_element_type=jnp.float32)
    shape = (EXAMPLES, SEQ_LEN, KP)
    down_feat = jnp.einsum('eto,eti->eoi', out_down.reshape(shape), in_down.reshape(shape), precision=top)
    up_feat = jnp.einsum('eto,eti->eoi', out_up.reshape(shape), in_up.reshape(shape), precision=top)
    scale = 1.0 / jnp.sqrt(lengths.astype(jnp.float32))
    features = jnp.concatenate([down_feat.reshape(EXAMPLES, KP * KP), up_feat.reshape(EXAMPLES, KP * KP)], axis=1) * scale[:, None]
    new_gram = gram + jnp.dot(features.T, features, precision=top) / EXAMPLES
    whitened = jnp.dot(inverse_factor, queries, precision=top)
    white_examples = jnp.dot(inverse_factor, features.T, precision=top)
    scores = jnp.dot(white_examples.T, whitened, precision=top) / jnp.sqrt(jnp.float32(K))
    return (new_gram, whitened, scores)
```

```python
import functools

import jax
import jax.numpy as jnp
from jax import lax
from jax.experimental import pallas as pl
from jax.experimental.pallas import tpu as pltpu
from jax.sharding import PartitionSpec as P

SEQ_LEN = 256
TILE = 256


def tokens_kernel(count, gates, with_up, idx, *refs):
    del idx
    cots, refs = refs[:count], refs[count:]
    weights, refs = refs[:count], refs[count:]
    gate_refs, refs = refs[:gates], refs[gates:]
    if with_up:
        up, refs = refs[0], refs[1:]
    proj, out = refs

    @pl.when(pl.program_id(0) == 0)
    def _():
        out[...] = jnp.zeros_like(out)

    grad = None
    for cot, weight in zip(cots, weights):
        term = lax.dot_general(
            cot[...], weight[...], (((1,), (1,)), ((), ())), preferred_element_type=jnp.float32
        )
        grad = term if grad is None else grad + term
    gate = gate_refs[0][...].astype(jnp.float32)
    for other in gate_refs[1:]:
        gate = gate + other[...].astype(jnp.float32)
    smooth = gate * jax.nn.sigmoid(gate)
    grad_up = (grad * smooth).astype(jnp.bfloat16)
    side = jnp.dot(grad_up, proj[...], preferred_element_type=jnp.float32)
    if with_up:
        hidden = (smooth * up[...].astype(jnp.float32)).astype(jnp.bfloat16)
        lanes = lax.broadcasted_iota(jnp.int32, side.shape, 1)
        left = jnp.dot(hidden, proj[...], preferred_element_type=jnp.float32)
        side = jnp.where(lanes < side.shape[1] // 2, left, side)
    out[...] += side


def tokens(idx, cot, weights, gate_parts, up, proj, first, tiles):
    count = len(weights)
    rows = cot.shape[0]
    width = weights[0].shape[1]
    in_specs = [
        pl.BlockSpec(
            (rows, width), functools.partial(lambda k, i, ix: (0, ix[k]), k), pipeline_mode=pl.Buffered(1)
        )
        for k in range(count)
    ]
    in_specs += [pl.BlockSpec((TILE, width), lambda i, ix: (first + i, 0)) for _ in weights]
    for _, start in gate_parts:
        in_specs.append(pl.BlockSpec((rows, TILE), functools.partial(lambda a, i, ix: (0, a + i), start)))
    operands = [cot] * count + list(weights) + [part for part, _ in gate_parts]
    if up is not None:
        in_specs.append(pl.BlockSpec((rows, TILE), lambda i, ix: (0, first + i)))
        operands.append(up)
    in_specs.append(pl.BlockSpec((TILE, proj.shape[1]), lambda i, ix: (first + i, 0)))
    operands.append(proj)
    return pl.pallas_call(
        functools.partial(tokens_kernel, count, len(gate_parts), up is not None),
        out_shape=jax.ShapeDtypeStruct((rows, proj.shape[1]), jnp.float32),
        grid_spec=pltpu.PrefetchScalarGridSpec(
            num_scalar_prefetch=1,
            grid=(tiles,),
            in_specs=in_specs,
            out_specs=pl.BlockSpec((rows, proj.shape[1]), lambda i, ix: (0, 0)),
        ),
        compiler_params=pltpu.CompilerParams(dimension_semantics=("arbitrary",)),
        cost_estimate=pl.CostEstimate(
            flops=2 * rows * TILE * tiles * (count * width + 256),
            bytes_accessed=TILE * tiles * (count * width + 2 * rows) * 2 + rows * count * width * 2,
            transcendentals=rows * TILE * tiles,
        ),
    )(idx, *operands)


def local(
    n,
    m,
    inputs,
    cotangent,
    gate_pre,
    up_pre,
    down_weight,
    proj_model,
    proj_hidden,
    lengths,
    gram,
    inverse_factor,
    queries,
):
    top = lax.Precision.HIGHEST
    f32 = jnp.float32
    f = lax.axis_index("fsdp")
    s = lax.axis_index("solve")
    rows = inputs.shape[0]
    local_seqs = lengths.shape[0]
    half = proj_model.shape[1] // 2
    h = n // 2
    chips = n // 2
    side = f // h

    def swap(x, axis, size, bit):
        return lax.ppermute(x, axis, [(i, i ^ bit) for i in range(size)])

    mirror_of = [(chips - 1 - i // 2) * 2 + i % 2 for i in range(n)]

    def mirror(x, keep=lambda chip: True):
        pairs = [(i, mirror_of[i]) for i in range(n) if keep(i // 2)]
        return lax.ppermute(x, "fsdp", pairs)

    def inner(chip):
        return chips // 4 <= chip < chips - chips // 4

    blocks = {0: down_weight}
    step = 2
    while step < h:
        blocks.update({k ^ step: swap(v, "fsdp", n, step) for k, v in list(blocks.items())})
        step *= 2
    gate_inner = mirror(gate_pre, inner)
    if h > 1:
        blocks.update({k ^ 1: swap(v, "fsdp", n, 1) for k, v in list(blocks.items())})
    order = sorted(blocks)
    weights = [blocks[k] for k in order]
    cot_full = lax.all_gather(cotangent, "solve", axis=1, tiled=True)
    part = rows // m
    near = cot_full.shape[1] // 2
    quarter = lax.dynamic_slice(cot_full, (s * part, (1 - side) * near), (part, near))
    cot_far = lax.all_gather(mirror(quarter), "solve", axis=0, tiled=True)
    tiles = gate_pre.shape[1] // TILE
    share = -(-tiles // 4)
    cuts = list(range(0, tiles, share)) + [tiles]
    gate_outer = [
        mirror(gate_pre[:, a * TILE : b * TILE], lambda chip: not inner(chip))
        for a, b in zip(cuts[:-1], cuts[1:])
    ]

    query_block = lax.all_gather(queries, "fsdp", axis=1, tiled=True)
    whitened = lax.psum_scatter(
        jnp.dot(inverse_factor, query_block, precision=top), "solve", scatter_dimension=0, tiled=True
    )
    whitened_rows = lax.all_gather(whitened, "solve", axis=0, tiled=True)
    query_side = lax.dot_general(inverse_factor, whitened_rows, (((0,), (0,)), ((), ())), precision=top)

    own_idx = jnp.stack([f ^ k for k in order]).astype(jnp.int32)
    far_idx = own_idx - side * h
    own = tokens(own_idx, cot_full, weights, [(gate_pre, 0)], up_pre, proj_hidden, 0, tiles)
    early = jnp.concatenate(
        [
            own[:, :half],
            jnp.dot(cotangent, proj_model[:, :half], preferred_element_type=f32),
            jnp.dot(inputs, proj_model[:, half:], preferred_element_type=f32),
        ],
        axis=1,
    )
    early = lax.psum(early, "solve")
    token_index = lax.broadcasted_iota(jnp.int32, (rows, 1), 0)
    slots = lax.broadcasted_iota(jnp.int32, (1, local_seqs), 1)
    length_of = jnp.sum(
        jnp.where(token_index // SEQ_LEN == slots, lengths[None, :], 0), axis=1, keepdims=True
    )
    weight_of = jnp.where(
        token_index % SEQ_LEN < length_of, 1.0 / jnp.sqrt(length_of.astype(f32)), 0.0
    )
    in_down = early[:, :half]
    out_down = early[:, half : 2 * half] * weight_of
    in_up = early[:, 2 * half :] * weight_of
    in_up_far = mirror(in_up)

    def pair(outs, ins):
        shape = (local_seqs, SEQ_LEN, half)
        feat = jnp.einsum("eto,eti->eoi", outs.reshape(shape), ins.reshape(shape), precision=top)
        return feat.reshape(local_seqs, half * half)

    down_all = lax.all_gather(pair(out_down, in_down), "fsdp", axis=0, tiled=True)
    up_own = pair(own[:, half:], in_up)

    far = None
    for a, b, outer in zip(cuts[:-1], cuts[1:], gate_outer):
        term = tokens(far_idx, cot_far, weights, [(gate_inner, a), (outer, 0)], None, proj_hidden, a, b - a)
        far = term if far is None else far + term
    up_far = pair(far[:, half:], in_up_far)
    up = jnp.concatenate([up_own, up_far], axis=0)
    bit = 1
    while bit < m:
        up = up + swap(up, "solve", m, bit)
        bit *= 2
    up_all = lax.all_gather(up, "fsdp", axis=0)
    mirrored = up_all[:, local_seqs:].reshape(chips, 2, local_seqs, half * half)[::-1]
    up_all = up_all[:, :local_seqs] + mirrored.reshape(n, local_seqs, half * half)
    all_features = jnp.concatenate([down_all, up_all.reshape(n * local_seqs, half * half)], axis=1)

    examples = all_features.shape[0]
    row_width = gram.shape[0]
    col_width = gram.shape[1]
    left = lax.dynamic_slice_in_dim(all_features, f * row_width, row_width, 1)
    right = lax.dynamic_slice_in_dim(all_features, s * col_width, col_width, 1)
    total = all_features.shape[1]
    scores = jnp.dot(right, query_side, precision=top) / jnp.sqrt(f32(total))
    for axis, size in (("fsdp", n), ("solve", m)):
        bit = 1
        while bit < size:
            scores = scores + swap(scores, axis, size, bit)
            bit *= 2
    new_gram = (
        gram + lax.dot_general(left, right, (((0,), (0,)), ((), ())), precision=top) / examples
    )
    return (new_gram, whitened, scores)


def solution(mesh):
    in_specs = (
        P("fsdp", "solve"),
        P("fsdp", "solve"),
        P("fsdp", "solve"),
        P("fsdp", "solve"),
        P("solve", "fsdp"),
        P("solve", None),
        P("solve", None),
        P("fsdp"),
        P("fsdp", "solve"),
        P("fsdp", "solve"),
        P("solve", "fsdp"),
    )
    out_specs = (P("fsdp", "solve"), P(("fsdp", "solve"), None), P())
    body = functools.partial(local, mesh.shape["fsdp"], mesh.shape["solve"])
    return jax.shard_map(body, mesh=mesh, in_specs=in_specs, out_specs=out_specs, check_vma=False)
```

```python
import functools

import jax
import jax.numpy as jnp
from jax import lax
from jax.experimental import pallas as pl
from jax.experimental.pallas import tpu as pltpu
from jax.sharding import PartitionSpec as P


SEQ_LEN = 256
TILE = 256


def tokens_kernel(count, gates, chained, idx, *refs):
    del idx
    cots, refs = refs[:count], refs[count:]
    weights, refs = refs[:count], refs[count:]
    gate_refs, refs = refs[:gates], refs[gates:]
    if chained:
        start, refs = refs[0], refs[1:]
    proj, out = refs

    @pl.when(pl.program_id(0) == 0)
    def _():
        out[...] = start[...] if chained else jnp.zeros_like(out)

    grad = None
    for cot, weight in zip(cots, weights):
        term = lax.dot_general(
            cot[...], weight[...], (((1,), (1,)), ((), ())), preferred_element_type=jnp.float32
        )
        grad = term if grad is None else grad + term
    gate = gate_refs[0][...].astype(jnp.float32)
    for other in gate_refs[1:]:
        gate = gate + other[...].astype(jnp.float32)
    smooth = gate * jax.nn.sigmoid(gate)
    grad_up = (grad * smooth).astype(jnp.bfloat16)
    out[...] += jnp.dot(grad_up, proj[...], preferred_element_type=jnp.float32)


def tokens(idx, cot, weights, gate_parts, start, proj, first, tiles):
    count = len(weights)
    rows = cot.shape[0]
    width = weights[0].shape[1]
    in_specs = [
        pl.BlockSpec(
            (rows, width), functools.partial(lambda k, i, ix: (0, ix[k]), k), pipeline_mode=pl.Buffered(1)
        )
        for k in range(count)
    ]
    in_specs += [pl.BlockSpec((TILE, width), lambda i, ix: (first + i, 0)) for _ in weights]
    for _, shift in gate_parts:
        in_specs.append(pl.BlockSpec((rows, TILE), functools.partial(lambda a, i, ix: (0, a + i), shift)))
    operands = [cot] * count + list(weights) + [part for part, _ in gate_parts]
    whole = pl.BlockSpec((rows, proj.shape[1]), lambda i, ix: (0, 0))
    if start is not None:
        in_specs.append(whole)
        operands.append(start)
    in_specs.append(pl.BlockSpec((TILE, proj.shape[1]), lambda i, ix: (first + i, 0)))
    operands.append(proj)
    return pl.pallas_call(
        functools.partial(tokens_kernel, count, len(gate_parts), start is not None),
        out_shape=jax.ShapeDtypeStruct((rows, proj.shape[1]), jnp.float32),
        grid_spec=pltpu.PrefetchScalarGridSpec(
            num_scalar_prefetch=1,
            grid=(tiles,),
            in_specs=in_specs,
            out_specs=whole,
        ),
        compiler_params=pltpu.CompilerParams(dimension_semantics=("arbitrary",)),
        cost_estimate=pl.CostEstimate(
            flops=2 * rows * TILE * tiles * (count * width + 256),
            bytes_accessed=TILE * tiles * (count * width + 2 * rows) * 2 + rows * count * width * 2,
            transcendentals=rows * TILE * tiles,
        ),
    )(idx, *operands)


def features_kernel(examples, seqs, mirror_of, idx, up, down, other, left_out, right_out, scores):
    f32 = jnp.float32
    pick = lax.broadcasted_iota(jnp.int32, (examples, up.shape[0]), 1)
    row = lax.broadcasted_iota(jnp.int32, (examples, up.shape[0]), 0)
    sel = jnp.zeros(pick.shape, f32)
    for i, j in enumerate(mirror_of):
        for e in range(seqs):
            hit = (pick == 2 * seqs * i + e) | (pick == 2 * seqs * j + seqs + e)
            sel = jnp.where(hit & (row == seqs * i + e), 1.0, sel)
    sel = sel.astype(jnp.bfloat16)

    def split(x):
        high = x.astype(jnp.bfloat16)
        return high, (x - high.astype(f32)).astype(jnp.bfloat16)

    def part(offset, width):
        size = down.shape[1]

        def from_up():
            at = pl.multiple_of(offset - size, 128)
            high, low = split(up[:, pl.ds(at, width)])
            return jnp.dot(sel, high, preferred_element_type=f32) + jnp.dot(
                sel, low, preferred_element_type=f32
            )

        def from_down():
            return down[:, pl.ds(pl.multiple_of(offset, 128), width)]

        return lax.cond(offset >= size, from_up, from_down)

    high, low = split(part(idx[0], left_out.shape[1]))
    left_out[...] = jnp.concatenate([high, low, high], axis=0)
    right = part(idx[1], right_out.shape[1])
    high, low = split(right)
    right_out[...] = jnp.concatenate([high, high, low], axis=0)
    scores[...] = jnp.dot(right, other[...], precision=lax.Precision.HIGHEST, preferred_element_type=f32)


def gram_kernel(scale, gram, left, right, out):
    term = lax.dot_general(
        left[...], right[...], (((0,), (0,)), ((), ())), preferred_element_type=jnp.float32
    )
    out[...] = gram[...] + term * scale


def local(
    n,
    m,
    inputs,
    cotangent,
    gate_pre,
    up_pre,
    down_weight,
    proj_model,
    proj_hidden,
    lengths,
    gram,
    inverse_factor,
    queries,
):
    top = lax.Precision.HIGHEST
    f32 = jnp.float32
    f = lax.axis_index("fsdp")
    s = lax.axis_index("solve")
    rows = inputs.shape[0]
    local_seqs = lengths.shape[0]
    half = proj_model.shape[1] // 2
    h = n // 2
    chips = n // 2
    side = f // h

    def swap(x, axis, size, bit):
        return lax.ppermute(x, axis, [(i, i ^ bit) for i in range(size)])

    mirror_of = [(chips - 1 - i // 2) * 2 + i % 2 for i in range(n)]

    def mirror(x, keep=lambda chip: True):
        pairs = [(i, mirror_of[i]) for i in range(n) if keep(i // 2)]
        return lax.ppermute(x, "fsdp", pairs)

    def inner(chip):
        return chips // 4 <= chip < chips - chips // 4

    blocks = {0: down_weight}
    step = 2
    while step < h:
        blocks.update({k ^ step: swap(v, "fsdp", n, step) for k, v in list(blocks.items())})
        step *= 2
    gate_inner = mirror(gate_pre, inner)
    blocks.update({k ^ 1: swap(v, "fsdp", n, 1) for k, v in list(blocks.items())})
    order = sorted(blocks)
    weights = [blocks[k] for k in order]
    cot_full = lax.all_gather(cotangent, "solve", axis=1, tiled=True)
    part = rows // m
    near = cot_full.shape[1] // 2
    quarter = lax.dynamic_slice(cot_full, (s * part, (1 - side) * near), (part, near))
    quarter = mirror(quarter)
    cot_far = lax.all_gather(quarter, "solve", axis=0, tiled=True)
    tiles = gate_pre.shape[1] // TILE
    share = -(-tiles // 4)
    cuts = list(range(0, tiles, share)) + [tiles]
    gate_outer = []
    for a, b in zip(cuts[:-1], cuts[1:]):
        gate_outer.append(mirror(gate_pre[:, a * TILE : b * TILE], lambda chip: not inner(chip)))

    gate = gate_pre.astype(f32)
    hidden = (gate * jax.nn.sigmoid(gate) * up_pre.astype(f32)).astype(jnp.bfloat16)
    early = jnp.concatenate(
        [
            jnp.dot(hidden, proj_hidden[:, :half], preferred_element_type=f32),
            jnp.dot(cotangent, proj_model[:, :half], preferred_element_type=f32),
            jnp.dot(inputs, proj_model[:, half:], preferred_element_type=f32),
        ],
        axis=1,
    )
    early = lax.psum(early, "solve")

    query_block = lax.all_gather(queries, "fsdp", axis=1, tiled=True)
    partial = jnp.dot(inverse_factor, query_block, precision=top)
    whitened = partial
    bit = m // 2
    while bit:
        size = whitened.shape[0] // 2
        mine = s // bit % 2
        moved = swap(lax.dynamic_slice_in_dim(whitened, (1 - mine) * size, size, 0), "solve", m, bit)
        whitened = lax.dynamic_slice_in_dim(whitened, mine * size, size, 0) + moved
        bit //= 2
    whitened_rows = whitened
    bit = 1
    while bit < m:
        mine = s // bit % 2
        moved = swap(whitened_rows, "solve", m, bit)
        whitened_rows = jnp.where(
            mine == 0,
            jnp.concatenate([whitened_rows, moved], axis=0),
            jnp.concatenate([moved, whitened_rows], axis=0),
        )
        bit *= 2
    query_side = lax.dot_general(
        inverse_factor, whitened_rows, (((0,), (0,)), ((), ())), precision=top
    )

    own_idx = jnp.stack([f ^ k for k in order]).astype(jnp.int32)
    far_idx = own_idx - side * h
    own = tokens(own_idx, cot_full, weights, [(gate_pre, 0)], None, proj_hidden, 0, tiles)
    token_index = lax.broadcasted_iota(jnp.int32, (rows, 1), 0)
    slots = lax.broadcasted_iota(jnp.int32, (1, local_seqs), 1)
    length_of = jnp.sum(
        jnp.where(token_index // SEQ_LEN == slots, lengths[None, :], 0), axis=1, keepdims=True
    )
    weight_of = jnp.where(
        token_index % SEQ_LEN < length_of, 1.0 / jnp.sqrt(length_of.astype(f32)), 0.0
    )
    in_down = early[:, :half]
    out_down = early[:, half : 2 * half] * weight_of
    in_up = early[:, 2 * half :] * weight_of
    in_up_far = mirror(in_up)

    def pair(outs, ins):
        shape = (local_seqs, SEQ_LEN, half)
        feat = jnp.einsum("eto,eti->eoi", outs.reshape(shape), ins.reshape(shape), precision=top)
        return feat.reshape(local_seqs, half * half)

    down_all = lax.all_gather(pair(out_down, in_down), "fsdp", axis=0, tiled=True)
    up_own = pair(own[:, half:], in_up)

    far = None
    for j, (a, b, outer) in enumerate(zip(cuts[:-1], cuts[1:], gate_outer)):
        if j == len(gate_outer) // 2:
            far_idx, query_side = lax.optimization_barrier((far_idx, query_side))
        far = tokens(far_idx, cot_far, weights, [(gate_inner, a), (outer, 0)], far, proj_hidden, a, b - a)
    up_far = pair(far[:, half:], in_up_far)
    up = jnp.concatenate([up_own, up_far], axis=0)
    bit = 1
    while bit < m:
        up = up + swap(up, "solve", m, bit)
        bit *= 2
    up_all = lax.all_gather(up, "fsdp", axis=0, tiled=True)

    examples = n * local_seqs
    row_width = gram.shape[0]
    col_width = gram.shape[1]
    count = queries.shape[1] * n
    at = jnp.stack([f * row_width, s * col_width]).astype(jnp.int32)
    left, right, scores = pl.pallas_call(
        functools.partial(features_kernel, examples, local_seqs, mirror_of),
        out_shape=(
            jax.ShapeDtypeStruct((3 * examples, row_width), jnp.bfloat16),
            jax.ShapeDtypeStruct((3 * examples, col_width), jnp.bfloat16),
            jax.ShapeDtypeStruct((examples, count), f32),
        ),
        in_specs=[pl.BlockSpec(memory_space=pltpu.SMEM)] + [pl.BlockSpec(memory_space=pltpu.VMEM)] * 3,
    )(at, up_all, down_all, query_side)
    total = 2 * half * half
    scores = scores / jnp.sqrt(f32(total))
    for axis, size in (("fsdp", n), ("solve", m)):
        bit = 1
        while bit < size:
            scores = scores + swap(scores, axis, size, bit)
            bit *= 2
    block = 128
    new_gram = pl.pallas_call(
        functools.partial(gram_kernel, 1.0 / examples),
        out_shape=jax.ShapeDtypeStruct(gram.shape, f32),
        grid=(row_width // block,),
        in_specs=[
            pl.BlockSpec((block, col_width), lambda i: (i, 0)),
            pl.BlockSpec((3 * examples, block), lambda i: (0, i)),
            pl.BlockSpec((3 * examples, col_width), lambda i: (0, 0)),
        ],
        out_specs=pl.BlockSpec((block, col_width), lambda i: (i, 0)),
    )(gram, left, right)
    return (new_gram, whitened, scores)


def solution(mesh):
    in_specs = (
        P("fsdp", "solve"),
        P("fsdp", "solve"),
        P("fsdp", "solve"),
        P("fsdp", "solve"),
        P("solve", "fsdp"),
        P("solve", None),
        P("solve", None),
        P("fsdp"),
        P("fsdp", "solve"),
        P("fsdp", "solve"),
        P("solve", "fsdp"),
    )
    out_specs = (P("fsdp", "solve"), P(("fsdp", "solve"), None), P())

    def body(*args):
        return local(mesh.shape["fsdp"], mesh.shape["solve"], *args)

    return jax.shard_map(body, mesh=mesh, in_specs=in_specs, out_specs=out_specs, check_vma=False)
```

```python
import functools

import jax
import jax.numpy as jnp
from jax import lax
from jax.experimental import pallas as pl
from jax.experimental.pallas import tpu as pltpu
from jax.sharding import PartitionSpec as P


SEQ_LEN = 256
TILE = 256


def tokens_kernel(count, gates, chained, idx, *refs):
    del idx
    cots, refs = refs[:count], refs[count:]
    weights, refs = refs[:count], refs[count:]
    gate_refs, refs = refs[:gates], refs[gates:]
    if chained:
        start, refs = refs[0], refs[1:]
    proj, out = refs

    @pl.when(pl.program_id(0) == 0)
    def _():
        out[...] = start[...] if chained else jnp.zeros_like(out)

    grad = None
    for cot, weight in zip(cots, weights):
        term = lax.dot_general(
            cot[...], weight[...], (((1,), (1,)), ((), ())), preferred_element_type=jnp.float32
        )
        grad = term if grad is None else grad + term
    gate = gate_refs[0][...].astype(jnp.float32)
    for other in gate_refs[1:]:
        gate = gate + other[...].astype(jnp.float32)
    smooth = gate * jax.nn.sigmoid(gate)
    grad_up = (grad * smooth).astype(jnp.bfloat16)
    out[...] += jnp.dot(grad_up, proj[...], preferred_element_type=jnp.float32)


def tokens(idx, cot, weights, gate_parts, start, proj, first, tiles):
    count = len(weights)
    rows = cot.shape[0]
    width = weights[0][0].shape[1]
    in_specs = [
        pl.BlockSpec(
            (rows, width), functools.partial(lambda k, i, ix: (0, ix[k]), k), pipeline_mode=pl.Buffered(1)
        )
        for k in range(count)
    ]
    for _, shift in weights:
        in_specs.append(pl.BlockSpec((TILE, width), functools.partial(lambda a, i, ix: (a + i, 0), shift)))
    for _, shift in gate_parts:
        in_specs.append(pl.BlockSpec((rows, TILE), functools.partial(lambda a, i, ix: (0, a + i), shift)))
    operands = [cot] * count + [part for part, _ in weights] + [part for part, _ in gate_parts]
    whole = pl.BlockSpec((rows, proj.shape[1]), lambda i, ix: (0, 0))
    if start is not None:
        in_specs.append(whole)
        operands.append(start)
    in_specs.append(pl.BlockSpec((TILE, proj.shape[1]), lambda i, ix: (first + i, 0)))
    operands.append(proj)
    return pl.pallas_call(
        functools.partial(tokens_kernel, count, len(gate_parts), start is not None),
        out_shape=jax.ShapeDtypeStruct((rows, proj.shape[1]), jnp.float32),
        grid_spec=pltpu.PrefetchScalarGridSpec(
            num_scalar_prefetch=1,
            grid=(tiles,),
            in_specs=in_specs,
            out_specs=whole,
        ),
        compiler_params=pltpu.CompilerParams(dimension_semantics=("arbitrary",)),
        cost_estimate=pl.CostEstimate(
            flops=2 * rows * TILE * tiles * (count * width + 256),
            bytes_accessed=TILE * tiles * (count * width + 2 * rows) * 2 + rows * count * width * 2,
            transcendentals=rows * TILE * tiles,
        ),
    )(idx, *operands)


def features_kernel(examples, seqs, mirror_of, idx, up, down, other, left_out, right_out, scores):
    f32 = jnp.float32
    pick = lax.broadcasted_iota(jnp.int32, (examples, up.shape[0]), 1)
    row = lax.broadcasted_iota(jnp.int32, (examples, up.shape[0]), 0)
    sel = jnp.zeros(pick.shape, f32)
    for i, j in enumerate(mirror_of):
        for e in range(seqs):
            hit = (pick == 2 * seqs * i + e) | (pick == 2 * seqs * j + seqs + e)
            sel = jnp.where(hit & (row == seqs * i + e), 1.0, sel)
    sel = sel.astype(jnp.bfloat16)

    def split(x):
        high = x.astype(jnp.bfloat16)
        return high, (x - high.astype(f32)).astype(jnp.bfloat16)

    def part(offset, width):
        size = down.shape[1]

        def from_up():
            at = pl.multiple_of(offset - size, 128)
            high, low = split(up[:, pl.ds(at, width)])
            return jnp.dot(sel, high, preferred_element_type=f32) + jnp.dot(
                sel, low, preferred_element_type=f32
            )

        def from_down():
            return down[:, pl.ds(pl.multiple_of(offset, 128), width)]

        return lax.cond(offset >= size, from_up, from_down)

    high, low = split(part(idx[0], left_out.shape[1]))
    left_out[...] = jnp.concatenate([high, low, high], axis=0)
    right = part(idx[1], right_out.shape[1])
    high, low = split(right)
    right_out[...] = jnp.concatenate([high, high, low], axis=0)
    scores[...] = jnp.dot(right, other[...], precision=lax.Precision.HIGHEST, preferred_element_type=f32)


def gram_kernel(scale, gram, left, right, *refs):
    out = refs[-1]
    term = lax.dot_general(
        left[...], right[...], (((0,), (0,)), ((), ())), preferred_element_type=jnp.float32
    )
    out[...] = gram[...] + term * scale


def local(
    n,
    m,
    inputs,
    cotangent,
    gate_pre,
    up_pre,
    down_weight,
    proj_model,
    proj_hidden,
    lengths,
    gram,
    inverse_factor,
    queries,
):
    top = lax.Precision.HIGHEST
    f32 = jnp.float32
    f = lax.axis_index("fsdp")
    s = lax.axis_index("solve")
    rows = inputs.shape[0]
    local_seqs = lengths.shape[0]
    half = proj_model.shape[1] // 2
    h = n // 2
    chips = n // 2
    side = f // h

    def swap(x, axis, size, bit):
        return lax.ppermute(x, axis, [(i, i ^ bit) for i in range(size)])

    mirror_of = [(chips - 1 - i // 2) * 2 + i % 2 for i in range(n)]

    def mirror(x, keep=lambda chip: True):
        pairs = [(i, mirror_of[i]) for i in range(n) if keep(i // 2)]
        return lax.ppermute(x, "fsdp", pairs)

    def inner(chip):
        return chips // 4 <= chip < chips - chips // 4

    gate_outer = mirror(gate_pre, lambda chip: not inner(chip))
    cot_full = lax.all_gather(cotangent, "solve", axis=1, tiled=True)
    part = rows // m
    near = cot_full.shape[1] // 2
    quarter = lax.dynamic_slice(cot_full, (s * part, (1 - side) * near), (part, near))
    quarter = mirror(quarter)
    cot_far = lax.all_gather(quarter, "solve", axis=0, tiled=True)
    tiles = gate_pre.shape[1] // TILE
    share = max(1, tiles // 7)
    cuts = [0, tiles - 3 * share, tiles - share, tiles]
    sibling = swap(down_weight, "fsdp", n, 1) if h > 1 else None
    chunks = []
    for j, (a, b) in enumerate(zip(cuts[:-1], cuts[1:])):
        blocks = {0: down_weight[a * TILE : b * TILE]}
        step = 2
        while step < h:
            blocks.update({k ^ step: swap(v, "fsdp", n, step) for k, v in list(blocks.items())})
            step *= 2
        gate_inner = mirror(gate_pre[:, a * TILE : b * TILE], inner)
        blocks.update({k ^ 1: swap(v, "fsdp", n, 1) for k, v in list(blocks.items()) if k})
        parts = {k: (v, 0) for k, v in blocks.items()}
        parts[0] = (down_weight, a)
        if h > 1:
            parts[1] = (sibling, a)
        order = sorted(parts)
        chunks.append((j, a, b, [parts[k] for k in order], gate_inner))

    gate = gate_pre.astype(f32)
    hidden = (gate * jax.nn.sigmoid(gate) * up_pre.astype(f32)).astype(jnp.bfloat16)
    early = jnp.concatenate(
        [
            jnp.dot(hidden, proj_hidden[:, :half], preferred_element_type=f32),
            jnp.dot(cotangent, proj_model[:, :half], preferred_element_type=f32),
            jnp.dot(inputs, proj_model[:, half:], preferred_element_type=f32),
        ],
        axis=1,
    )
    bit = 1
    while bit < m:
        early = early + swap(early, "solve", m, bit)
        bit *= 2

    query_block = lax.all_gather(queries, "fsdp", axis=1, tiled=True)
    partial = jnp.dot(inverse_factor, query_block, precision=top)
    whitened = partial
    bit = m // 2
    while bit:
        size = whitened.shape[0] // 2
        mine = s // bit % 2
        moved = swap(lax.dynamic_slice_in_dim(whitened, (1 - mine) * size, size, 0), "solve", m, bit)
        whitened = lax.dynamic_slice_in_dim(whitened, mine * size, size, 0) + moved
        bit //= 2
    whitened_rows = whitened
    bit = 1
    while bit < m:
        mine = s // bit % 2
        moved = swap(whitened_rows, "solve", m, bit)
        whitened_rows = jnp.where(
            mine == 0,
            jnp.concatenate([whitened_rows, moved], axis=0),
            jnp.concatenate([moved, whitened_rows], axis=0),
        )
        bit *= 2
    query_side = lax.dot_general(
        inverse_factor, whitened_rows, (((0,), (0,)), ((), ())), precision=top
    )

    own_idx = jnp.stack([f ^ k for k in order]).astype(jnp.int32)
    far_idx = own_idx - side * h
    own = None
    for j, a, b, weights, _ in chunks:
        own = tokens(own_idx, cot_full, weights, [(gate_pre, a)], own, proj_hidden, a, b - a)
    token_index = lax.broadcasted_iota(jnp.int32, (rows, 1), 0)
    slots = lax.broadcasted_iota(jnp.int32, (1, local_seqs), 1)
    length_of = jnp.sum(
        jnp.where(token_index // SEQ_LEN == slots, lengths[None, :], 0), axis=1, keepdims=True
    )
    weight_of = jnp.where(
        token_index % SEQ_LEN < length_of, 1.0 / jnp.sqrt(length_of.astype(f32)), 0.0
    )
    in_down = early[:, :half]
    out_down = early[:, half : 2 * half] * weight_of
    in_up = early[:, 2 * half :] * weight_of
    in_up_far = mirror(in_up)

    def pair(outs, ins):
        shape = (local_seqs, SEQ_LEN, half)
        feat = jnp.einsum("eto,eti->eoi", outs.reshape(shape), ins.reshape(shape), precision=top)
        return feat.reshape(local_seqs, half * half)

    down_all = lax.all_gather(pair(out_down, in_down), "fsdp", axis=0, tiled=True)
    up_own = pair(own[:, half:], in_up)

    far = None
    for j, a, b, weights, gate_inner in chunks:
        if j == len(chunks) - 2:
            far_idx, query_side = lax.optimization_barrier((far_idx, query_side))
        gates = [(gate_outer, a), (gate_inner, 0)]
        far = tokens(far_idx, cot_far, weights, gates, far, proj_hidden, a, b - a)
    up_far = pair(far[:, half:], in_up_far)
    up = jnp.concatenate([up_own, up_far], axis=0)
    bit = 1
    while bit < m:
        up = up + swap(up, "solve", m, bit)
        bit *= 2
    up_all = lax.all_gather(up, "fsdp", axis=0, tiled=True)

    examples = n * local_seqs
    row_width = gram.shape[0]
    col_width = gram.shape[1]
    count = queries.shape[1] * n
    at = jnp.stack([f * row_width, s * col_width]).astype(jnp.int32)
    left, right, scores = pl.pallas_call(
        functools.partial(features_kernel, examples, local_seqs, mirror_of),
        out_shape=(
            jax.ShapeDtypeStruct((3 * examples, row_width), jnp.bfloat16),
            jax.ShapeDtypeStruct((3 * examples, col_width), jnp.bfloat16),
            jax.ShapeDtypeStruct((examples, count), f32),
        ),
        in_specs=[pl.BlockSpec(memory_space=pltpu.SMEM)] + [pl.BlockSpec(memory_space=pltpu.VMEM)] * 3,
    )(at, up_all, down_all, query_side)
    total = 2 * half * half
    scores = scores / jnp.sqrt(f32(total))
    for axis, size in (("fsdp", n), ("solve", m)):
        bit = 1
        while bit < size:
            scores = scores + swap(scores, axis, size, bit)
            bit *= 2
    block = 128
    steps = row_width // block
    ends = [0, steps // 2, steps]
    new_gram = None
    for a, b in zip(ends[:-1], ends[1:]):
        in_specs = [
            pl.BlockSpec((block, col_width), functools.partial(lambda z, i: (z + i, 0), a)),
            pl.BlockSpec((3 * examples, block), functools.partial(lambda z, i: (0, z + i), a)),
            pl.BlockSpec((3 * examples, col_width), lambda i: (0, 0)),
        ]
        operands = [gram, left, right]
        if new_gram is not None:
            in_specs.append(pl.BlockSpec(memory_space=pl.ANY))
            operands.append(new_gram)
        new_gram = pl.pallas_call(
            functools.partial(gram_kernel, 1.0 / examples),
            out_shape=jax.ShapeDtypeStruct(gram.shape, f32),
            grid=(b - a,),
            in_specs=in_specs,
            out_specs=pl.BlockSpec((block, col_width), functools.partial(lambda z, i: (z + i, 0), a)),
            input_output_aliases={} if new_gram is None else {3: 0},
        )(*operands)
    return (new_gram, whitened, scores)


def solution(mesh):
    in_specs = (
        P("fsdp", "solve"),
        P("fsdp", "solve"),
        P("fsdp", "solve"),
        P("fsdp", "solve"),
        P("solve", "fsdp"),
        P("solve", None),
        P("solve", None),
        P("fsdp"),
        P("fsdp", "solve"),
        P("fsdp", "solve"),
        P("solve", "fsdp"),
    )
    out_specs = (P("fsdp", "solve"), P(("fsdp", "solve"), None), P())

    def body(*args):
        return local(mesh.shape["fsdp"], mesh.shape["solve"], *args)

    return jax.shard_map(body, mesh=mesh, in_specs=in_specs, out_specs=out_specs, check_vma=False)
```

```python
import functools

import jax
import jax.numpy as jnp
from jax import lax
from jax.experimental import pallas as pl
from jax.experimental.pallas import tpu as pltpu
from jax.sharding import PartitionSpec as P


SEQ_LEN = 256
TILE = 256


def tokens_kernel(count, gates, chained, idx, *refs):
    del idx
    cots, refs = refs[:count], refs[count:]
    weights, refs = refs[:count], refs[count:]
    gate_refs, refs = refs[:gates], refs[gates:]
    if chained:
        start, refs = refs[0], refs[1:]
    proj, out = refs

    @pl.when(pl.program_id(0) == 0)
    def _():
        out[...] = start[...] if chained else jnp.zeros_like(out)

    grad = None
    for cot, weight in zip(cots, weights):
        term = lax.dot_general(
            cot[...], weight[...], (((1,), (1,)), ((), ())), preferred_element_type=jnp.float32
        )
        grad = term if grad is None else grad + term
    gate = gate_refs[0][...].astype(jnp.float32)
    for other in gate_refs[1:]:
        gate = gate + other[...].astype(jnp.float32)
    smooth = gate * jax.nn.sigmoid(gate)
    grad_up = (grad * smooth).astype(jnp.bfloat16)
    out[...] += jnp.dot(grad_up, proj[...], preferred_element_type=jnp.float32)


def tokens(idx, cot, weights, gate_parts, start, proj, first, tiles):
    count = len(weights)
    rows = cot.shape[0]
    width = weights[0][0].shape[1]
    in_specs = [
        pl.BlockSpec(
            (rows, width), functools.partial(lambda k, i, ix: (0, ix[k]), k), pipeline_mode=pl.Buffered(1)
        )
        for k in range(count)
    ]
    for _, shift in weights:
        in_specs.append(pl.BlockSpec((TILE, width), functools.partial(lambda a, i, ix: (a + i, 0), shift)))
    for _, shift in gate_parts:
        in_specs.append(pl.BlockSpec((rows, TILE), functools.partial(lambda a, i, ix: (0, a + i), shift)))
    operands = [cot] * count + [part for part, _ in weights] + [part for part, _ in gate_parts]
    whole = pl.BlockSpec((rows, proj.shape[1]), lambda i, ix: (0, 0))
    if start is not None:
        in_specs.append(whole)
        operands.append(start)
    in_specs.append(pl.BlockSpec((TILE, proj.shape[1]), lambda i, ix: (first + i, 0)))
    operands.append(proj)
    return pl.pallas_call(
        functools.partial(tokens_kernel, count, len(gate_parts), start is not None),
        out_shape=jax.ShapeDtypeStruct((rows, proj.shape[1]), jnp.float32),
        grid_spec=pltpu.PrefetchScalarGridSpec(
            num_scalar_prefetch=1,
            grid=(tiles,),
            in_specs=in_specs,
            out_specs=whole,
        ),
        compiler_params=pltpu.CompilerParams(dimension_semantics=("arbitrary",)),
        cost_estimate=pl.CostEstimate(
            flops=2 * rows * TILE * tiles * (count * width + 256),
            bytes_accessed=TILE * tiles * (count * width + 2 * rows) * 2 + rows * count * width * 2,
            transcendentals=rows * TILE * tiles,
        ),
    )(idx, *operands)


def features_kernel(examples, seqs, idx, both, other, left_out, right_out, scores):
    f32 = jnp.float32
    shape = (examples, both.shape[0])
    pick = lax.broadcasted_iota(jnp.int32, shape, 1)
    row = lax.broadcasted_iota(jnp.int32, shape, 0)
    up = jnp.zeros(shape, f32)
    down = jnp.zeros(shape, f32)
    for i in range(examples // seqs):
        for e in range(seqs):
            here = row == seqs * i + e
            up = jnp.where((pick == 2 * seqs * i + e) & here, 1.0, up)
            down = jnp.where((pick == 2 * seqs * i + seqs + e) & here, 1.0, down)

    def split(x):
        high = x.astype(jnp.bfloat16)
        return high, (x - high.astype(f32)).astype(jnp.bfloat16)

    def part(offset, width):
        size = both.shape[1]
        is_up = offset >= size
        at = pl.multiple_of(offset - jnp.where(is_up, size, 0), 128)
        high, low = split(both[:, pl.ds(at, width)])
        sel = jnp.where(is_up, up, down).astype(jnp.bfloat16)
        return jnp.dot(sel, high, preferred_element_type=f32) + jnp.dot(sel, low, preferred_element_type=f32)

    high, low = split(part(idx[0], left_out.shape[1]))
    left_out[...] = jnp.concatenate([high, low, high], axis=0)
    right = part(idx[1], right_out.shape[1])
    high, low = split(right)
    right_out[...] = jnp.concatenate([high, high, low], axis=0)
    scores[...] = jnp.dot(right, other[...], precision=lax.Precision.HIGHEST, preferred_element_type=f32)


def gram_kernel(scale, gram, left, right, *refs):
    out = refs[-1]
    term = lax.dot_general(
        left[...], right[...], (((0,), (0,)), ((), ())), preferred_element_type=jnp.float32
    )
    out[...] = gram[...] + term * scale


def local(
    n,
    m,
    inputs,
    cotangent,
    gate_pre,
    up_pre,
    down_weight,
    proj_model,
    proj_hidden,
    lengths,
    gram,
    inverse_factor,
    queries,
):
    top = lax.Precision.HIGHEST
    f32 = jnp.float32
    f = lax.axis_index("fsdp")
    s = lax.axis_index("solve")
    rows = inputs.shape[0]
    local_seqs = lengths.shape[0]
    half = proj_model.shape[1] // 2
    h = n // 2
    chips = n // 2
    side = f // h

    def swap(x, axis, size, bit):
        return lax.ppermute(x, axis, [(i, i ^ bit) for i in range(size)])

    mirror_of = [(chips - 1 - i // 2) * 2 + i % 2 for i in range(n)]

    def mirror(x, keep=lambda chip: True):
        pairs = [(i, mirror_of[i]) for i in range(n) if keep(i // 2)]
        return lax.ppermute(x, "fsdp", pairs)

    def inner(chip):
        return chips // 4 <= chip < chips - chips // 4

    tiles = gate_pre.shape[1] // TILE
    first = tiles * 5 // 7 * TILE
    blocks = {0: down_weight}
    if h > 2:
        from_inner = lax.ppermute(down_weight, "fsdp", [(i, i ^ 2) for i in range(n) if inner(i // 2)])
        outer_pairs = [(i, i ^ 2) for i in range(n) if not inner(i // 2)]
        part_a = lax.ppermute(down_weight[:first], "fsdp", outer_pairs)
    gate_inner = mirror(gate_pre, inner)
    cot_full = lax.all_gather(cotangent, "solve", axis=1, tiled=True)
    part = rows // m
    near = cot_full.shape[1] // 2
    quarter = lax.dynamic_slice(cot_full, (s * part, (1 - side) * near), (part, near))
    quarter = mirror(quarter)
    cot_far = lax.all_gather(quarter, "solve", axis=0, tiled=True)
    if h > 2:
        part_b = lax.ppermute(down_weight[first:], "fsdp", outer_pairs)
        part_b, _ = lax.optimization_barrier((part_b, quarter))
        blocks[2] = from_inner + jnp.concatenate([part_a, part_b], axis=0)
    step = 4
    while step < h:
        blocks.update({k ^ step: swap(v, "fsdp", n, step) for k, v in list(blocks.items())})
        step *= 2
    if h > 1:
        blocks.update({k ^ 1: swap(v, "fsdp", n, 1) for k, v in list(blocks.items())})
    order = sorted(blocks)
    weights = [blocks[k] for k in order]
    share = max(1, tiles // 7)
    cuts = [0, tiles - 3 * share, tiles - share, tiles]
    chunks = []
    for j, (a, b) in enumerate(zip(cuts[:-1], cuts[1:])):
        gate_outer = mirror(gate_pre[:, a * TILE : b * TILE], lambda chip: not inner(chip))
        chunks.append((j, a, b, gate_outer))

    gate = gate_pre.astype(f32)
    hidden = (gate * jax.nn.sigmoid(gate) * up_pre.astype(f32)).astype(jnp.bfloat16)
    early = jnp.concatenate(
        [
            jnp.dot(hidden, proj_hidden[:, :half], preferred_element_type=f32),
            jnp.dot(cotangent, proj_model[:, :half], preferred_element_type=f32),
            jnp.dot(inputs, proj_model[:, half:], preferred_element_type=f32),
        ],
        axis=1,
    )
    bit = 1
    while bit < m:
        early = early + swap(early, "solve", m, bit)
        bit *= 2

    query_block = lax.all_gather(queries, "fsdp", axis=1, tiled=True)
    partial = jnp.dot(inverse_factor, query_block, precision=top)
    whitened = partial
    bit = m // 2
    while bit:
        size = whitened.shape[0] // 2
        mine = s // bit % 2
        moved = swap(lax.dynamic_slice_in_dim(whitened, (1 - mine) * size, size, 0), "solve", m, bit)
        whitened = lax.dynamic_slice_in_dim(whitened, mine * size, size, 0) + moved
        bit //= 2
    whitened_rows = whitened
    bit = 1
    while bit < m:
        mine = s // bit % 2
        moved = swap(whitened_rows, "solve", m, bit)
        whitened_rows = jnp.where(
            mine == 0,
            jnp.concatenate([whitened_rows, moved], axis=0),
            jnp.concatenate([moved, whitened_rows], axis=0),
        )
        bit *= 2
    query_side = lax.dot_general(
        inverse_factor, whitened_rows, (((0,), (0,)), ((), ())), precision=top
    )

    own_idx = jnp.stack([f ^ k for k in order]).astype(jnp.int32)
    far_idx = own_idx - side * h
    own = tokens(
        own_idx, cot_full, [(v, 0) for v in weights], [(gate_pre, 0)], None, proj_hidden, 0, tiles
    )
    token_index = lax.broadcasted_iota(jnp.int32, (rows, 1), 0)
    slots = lax.broadcasted_iota(jnp.int32, (1, local_seqs), 1)
    length_of = jnp.sum(
        jnp.where(token_index // SEQ_LEN == slots, lengths[None, :], 0), axis=1, keepdims=True
    )
    weight_of = jnp.where(
        token_index % SEQ_LEN < length_of, 1.0 / jnp.sqrt(length_of.astype(f32)), 0.0
    )
    in_down = early[:, :half]
    out_down = early[:, half : 2 * half] * weight_of
    in_up = early[:, 2 * half :] * weight_of
    in_up_far = mirror(in_up)

    def pair(outs, ins):
        shape = (local_seqs, SEQ_LEN, half)
        feat = jnp.einsum("eto,eti->eoi", outs.reshape(shape), ins.reshape(shape), precision=top)
        return feat.reshape(local_seqs, half * half)

    down = pair(out_down, in_down)
    up_own = pair(own[:, half:], in_up)

    far = None
    for j, a, b, gate_outer in chunks:
        if j == len(chunks) - 1:
            far_idx, query_side = lax.optimization_barrier((far_idx, query_side))
        gates = [(gate_inner, a), (gate_outer, 0)]
        far = tokens(far_idx, cot_far, [(v, a) for v in weights], gates, far, proj_hidden, a, b - a)
    up_far = pair(far[:, half:], in_up_far)
    up = up_own + mirror(up_far)
    bit = 1
    while bit < m:
        up = up + swap(up, "solve", m, bit)
        bit *= 2
    both = lax.all_gather(jnp.concatenate([up, down], axis=0), "fsdp", axis=0, tiled=True)

    examples = n * local_seqs
    row_width = gram.shape[0]
    col_width = gram.shape[1]
    count = queries.shape[1] * n
    at = jnp.stack([f * row_width, s * col_width]).astype(jnp.int32)
    left, right, scores = pl.pallas_call(
        functools.partial(features_kernel, examples, local_seqs),
        out_shape=(
            jax.ShapeDtypeStruct((3 * examples, row_width), jnp.bfloat16),
            jax.ShapeDtypeStruct((3 * examples, col_width), jnp.bfloat16),
            jax.ShapeDtypeStruct((examples, count), f32),
        ),
        in_specs=[pl.BlockSpec(memory_space=pltpu.SMEM)] + [pl.BlockSpec(memory_space=pltpu.VMEM)] * 2,
    )(at, both, query_side)
    total = 2 * half * half
    scores = scores / jnp.sqrt(f32(total))
    for axis, size in (("fsdp", n), ("solve", m)):
        bit = 1
        while bit < size:
            scores = scores + swap(scores, axis, size, bit)
            bit *= 2
    block = 128
    steps = row_width // block
    ends = [0, steps // 2, steps]
    new_gram = None
    for a, b in zip(ends[:-1], ends[1:]):
        in_specs = [
            pl.BlockSpec((block, col_width), functools.partial(lambda z, i: (z + i, 0), a)),
            pl.BlockSpec((3 * examples, block), functools.partial(lambda z, i: (0, z + i), a)),
            pl.BlockSpec((3 * examples, col_width), lambda i: (0, 0)),
        ]
        operands = [gram, left, right]
        if new_gram is not None:
            in_specs.append(pl.BlockSpec(memory_space=pl.ANY))
            operands.append(new_gram)
        new_gram = pl.pallas_call(
            functools.partial(gram_kernel, 1.0 / examples),
            out_shape=jax.ShapeDtypeStruct(gram.shape, f32),
            grid=(b - a,),
            in_specs=in_specs,
            out_specs=pl.BlockSpec((block, col_width), functools.partial(lambda z, i: (z + i, 0), a)),
            input_output_aliases={} if new_gram is None else {3: 0},
        )(*operands)
    return (new_gram, whitened, scores)


def solution(mesh):
    in_specs = (
        P("fsdp", "solve"),
        P("fsdp", "solve"),
        P("fsdp", "solve"),
        P("fsdp", "solve"),
        P("solve", "fsdp"),
        P("solve", None),
        P("solve", None),
        P("fsdp"),
        P("fsdp", "solve"),
        P("fsdp", "solve"),
        P("solve", "fsdp"),
    )
    out_specs = (P("fsdp", "solve"), P(("fsdp", "solve"), None), P())

    def body(*args):
        return local(mesh.shape["fsdp"], mesh.shape["solve"], *args)

    return jax.shard_map(body, mesh=mesh, in_specs=in_specs, out_specs=out_specs, check_vma=False)
```

```python
import functools

import jax
import jax.numpy as jnp
from jax import lax
from jax.experimental import pallas as pl
from jax.experimental.pallas import tpu as pltpu
from jax.sharding import PartitionSpec as P


SEQ_LEN = 256
TILE = 256


def tokens_kernel(count, gates, chained, idx, *refs):
    del idx
    cots, refs = refs[:count], refs[count:]
    weights, refs = refs[:count], refs[count:]
    gate_refs, refs = refs[:gates], refs[gates:]
    if chained:
        start, refs = refs[0], refs[1:]
    proj, out = refs

    @pl.when(pl.program_id(0) == 0)
    def _():
        out[...] = start[...] if chained else jnp.zeros_like(out)

    grad = None
    for cot, weight in zip(cots, weights):
        term = lax.dot_general(
            cot[...], weight[...], (((1,), (1,)), ((), ())), preferred_element_type=jnp.float32
        )
        grad = term if grad is None else grad + term
    gate = gate_refs[0][...].astype(jnp.float32)
    for other in gate_refs[1:]:
        gate = gate + other[...].astype(jnp.float32)
    smooth = gate * jax.nn.sigmoid(gate)
    grad_up = (grad * smooth).astype(jnp.bfloat16)
    out[...] += jnp.dot(grad_up, proj[...], preferred_element_type=jnp.float32)


def tokens(idx, cot, weights, gate_parts, start, proj, first, tiles):
    count = len(weights)
    rows = cot.shape[0]
    width = weights[0][0].shape[1]
    in_specs = [
        pl.BlockSpec(
            (rows, width), functools.partial(lambda k, i, ix: (0, ix[k]), k), pipeline_mode=pl.Buffered(1)
        )
        for k in range(count)
    ]
    for _, shift in weights:
        in_specs.append(pl.BlockSpec((TILE, width), functools.partial(lambda a, i, ix: (a + i, 0), shift)))
    for _, shift in gate_parts:
        in_specs.append(pl.BlockSpec((rows, TILE), functools.partial(lambda a, i, ix: (0, a + i), shift)))
    operands = [cot] * count + [part for part, _ in weights] + [part for part, _ in gate_parts]
    whole = pl.BlockSpec((rows, proj.shape[1]), lambda i, ix: (0, 0))
    if start is not None:
        in_specs.append(whole)
        operands.append(start)
    in_specs.append(pl.BlockSpec((TILE, proj.shape[1]), lambda i, ix: (first + i, 0)))
    operands.append(proj)
    return pl.pallas_call(
        functools.partial(tokens_kernel, count, len(gate_parts), start is not None),
        out_shape=jax.ShapeDtypeStruct((rows, proj.shape[1]), jnp.float32),
        grid_spec=pltpu.PrefetchScalarGridSpec(
            num_scalar_prefetch=1,
            grid=(tiles,),
            in_specs=in_specs,
            out_specs=whole,
        ),
        compiler_params=pltpu.CompilerParams(dimension_semantics=("arbitrary",)),
        cost_estimate=pl.CostEstimate(
            flops=2 * rows * TILE * tiles * (count * width + 256),
            bytes_accessed=TILE * tiles * (count * width + 2 * rows) * 2 + rows * count * width * 2,
            transcendentals=rows * TILE * tiles,
        ),
    )(idx, *operands)


def features_kernel(examples, seqs, idx, both, other, left_out, right_out, scores):
    f32 = jnp.float32
    shape = (examples, both.shape[0])
    pick = lax.broadcasted_iota(jnp.int32, shape, 1)
    row = lax.broadcasted_iota(jnp.int32, shape, 0)
    up = jnp.zeros(shape, f32)
    down = jnp.zeros(shape, f32)
    for i in range(examples // seqs):
        for e in range(seqs):
            here = row == seqs * i + e
            up = jnp.where((pick == 2 * seqs * i + e) & here, 1.0, up)
            down = jnp.where((pick == 2 * seqs * i + seqs + e) & here, 1.0, down)

    def split(x):
        high = x.astype(jnp.bfloat16)
        return high, (x - high.astype(f32)).astype(jnp.bfloat16)

    def part(offset, width):
        size = both.shape[1]
        is_up = offset >= size
        at = pl.multiple_of(offset - jnp.where(is_up, size, 0), 128)
        high, low = split(both[:, pl.ds(at, width)])
        sel = jnp.where(is_up, up, down).astype(jnp.bfloat16)
        return jnp.dot(sel, high, preferred_element_type=f32) + jnp.dot(sel, low, preferred_element_type=f32)

    high, low = split(part(idx[0], left_out.shape[1]))
    left_out[...] = jnp.concatenate([high, low, high], axis=0)
    right = part(idx[1], right_out.shape[1])
    high, low = split(right)
    right_out[...] = jnp.concatenate([high, high, low], axis=0)
    scores[...] = lax.dot_general(
        right,
        other[...],
        (((1,), (1,)), ((), ())),
        precision=lax.Precision.HIGHEST,
        preferred_element_type=f32,
    )


def gram_kernel(scale, gram, left, right, *refs):
    out = refs[-1]
    term = lax.dot_general(
        left[...], right[...], (((0,), (0,)), ((), ())), preferred_element_type=jnp.float32
    )
    out[...] = gram[...] + term * scale


def local(
    n,
    m,
    inputs,
    cotangent,
    gate_pre,
    up_pre,
    down_weight,
    proj_model,
    proj_hidden,
    lengths,
    gram,
    inverse_factor,
    queries,
):
    top = lax.Precision.HIGHEST
    f32 = jnp.float32
    f = lax.axis_index("fsdp")
    s = lax.axis_index("solve")
    rows = inputs.shape[0]
    local_seqs = lengths.shape[0]
    half = proj_model.shape[1] // 2
    h = n // 2
    chips = n // 2
    side = f // h

    def swap(x, axis, size, bit):
        return lax.ppermute(x, axis, [(i, i ^ bit) for i in range(size)])

    mirror_of = [(chips - 1 - i // 2) * 2 + i % 2 for i in range(n)]

    def mirror(x, keep=lambda chip: True):
        pairs = [(i, mirror_of[i]) for i in range(n) if keep(i // 2)]
        return lax.ppermute(x, "fsdp", pairs)

    def inner(chip):
        return chips // 4 <= chip < chips - chips // 4

    tiles = gate_pre.shape[1] // TILE
    blocks = {0: down_weight}
    step = 2
    while step < h:
        blocks.update({k ^ step: swap(v, "fsdp", n, step) for k, v in list(blocks.items())})
        step *= 2
    gate_inner = mirror(gate_pre, inner)
    cot_full = lax.all_gather(cotangent, "solve", axis=1, tiled=True)
    part = rows // m
    near = cot_full.shape[1] // 2
    quarter = lax.dynamic_slice(cot_full, (s * part, (1 - side) * near), (part, near))
    quarter = mirror(quarter)
    cot_far = lax.all_gather(quarter, "solve", axis=0, tiled=True)
    sibling = swap(down_weight, "fsdp", n, 1)
    blocks.update({k ^ 1: swap(v, "fsdp", n, 1) for k, v in list(blocks.items()) if k})
    blocks[1] = sibling
    order = sorted(blocks)
    weights = [blocks[k] for k in order]
    share = max(1, tiles // 7)
    cuts = [0, tiles - 3 * share, tiles - share, tiles]
    chunks = []
    for j, (a, b) in enumerate(zip(cuts[:-1], cuts[1:])):
        gate_outer, _ = lax.optimization_barrier((gate_pre[:, a * TILE : b * TILE], quarter))
        gate_outer = mirror(gate_outer, lambda chip: not inner(chip))
        chunks.append((j, a, b, gate_outer))

    gate = gate_pre.astype(f32)
    hidden = (gate * jax.nn.sigmoid(gate) * up_pre.astype(f32)).astype(jnp.bfloat16)
    early = jnp.concatenate(
        [
            jnp.dot(hidden, proj_hidden[:, :half], preferred_element_type=f32),
            jnp.dot(cotangent, proj_model[:, :half], preferred_element_type=f32),
            jnp.dot(inputs, proj_model[:, half:], preferred_element_type=f32),
        ],
        axis=1,
    )
    bit = 1
    while bit < m:
        early = early + swap(early, "solve", m, bit)
        bit *= 2

    query_block = lax.all_gather(queries.astype(jnp.bfloat16), "fsdp", axis=1, tiled=True)
    partial = jnp.dot(inverse_factor, query_block.astype(f32), precision=lax.Precision.HIGH)
    whitened = partial
    bit = m // 2
    while bit:
        size = whitened.shape[0] // 2
        mine = s // bit % 2
        moved = swap(lax.dynamic_slice_in_dim(whitened, (1 - mine) * size, size, 0), "solve", m, bit)
        whitened = lax.dynamic_slice_in_dim(whitened, mine * size, size, 0) + moved
        bit //= 2
    whitened_rows = whitened
    bit = 1
    while bit < m:
        mine = s // bit % 2
        moved = swap(whitened_rows, "solve", m, bit)
        whitened_rows = jnp.where(
            mine == 0,
            jnp.concatenate([whitened_rows, moved], axis=0),
            jnp.concatenate([moved, whitened_rows], axis=0),
        )
        bit *= 2
    query_side = lax.dot_general(whitened_rows, inverse_factor, (((0,), (0,)), ((), ())), precision=lax.Precision.HIGH)

    own_idx = jnp.stack([f ^ k for k in order]).astype(jnp.int32)
    far_idx = own_idx - side * h
    own = tokens(
        own_idx, cot_full, [(v, 0) for v in weights], [(gate_pre, 0)], None, proj_hidden, 0, tiles
    )
    token_index = lax.broadcasted_iota(jnp.int32, (rows, 1), 0)
    slots = lax.broadcasted_iota(jnp.int32, (1, local_seqs), 1)
    length_of = jnp.sum(
        jnp.where(token_index // SEQ_LEN == slots, lengths[None, :], 0), axis=1, keepdims=True
    )
    weight_of = jnp.where(
        token_index % SEQ_LEN < length_of, 1.0 / jnp.sqrt(length_of.astype(f32)), 0.0
    )
    in_down = early[:, :half]
    out_down = early[:, half : 2 * half] * weight_of
    in_up = early[:, 2 * half :] * weight_of
    in_up_far = mirror(in_up.astype(jnp.bfloat16)).astype(f32)

    def pair(outs, ins):
        shape = (local_seqs, SEQ_LEN, half)
        feat = jnp.einsum("eto,eti->eoi", outs.reshape(shape), ins.reshape(shape), precision=top)
        return feat.reshape(local_seqs, half * half)

    down = pair(out_down, in_down)
    up_own = pair(own[:, half:], in_up)

    far = None
    for j, a, b, gate_outer in chunks:
        if j == len(chunks) - 1:
            far_idx, query_side = lax.optimization_barrier((far_idx, query_side))
        gates = [(gate_inner, a), (gate_outer, 0)]
        far = tokens(far_idx, cot_far, [(v, a) for v in weights], gates, far, proj_hidden, a, b - a)
    up_far = pair(far[:, half:], in_up_far)
    up = up_own + mirror(up_far)
    bit = 1
    while bit < m:
        up = up + swap(up, "solve", m, bit)
        bit *= 2
    both = lax.all_gather(jnp.concatenate([up, down], axis=0), "fsdp", axis=0, tiled=True)

    examples = n * local_seqs
    row_width = gram.shape[0]
    col_width = gram.shape[1]
    count = queries.shape[1] * n
    at = jnp.stack([f * row_width, s * col_width]).astype(jnp.int32)
    left, right, scores = pl.pallas_call(
        functools.partial(features_kernel, examples, local_seqs),
        out_shape=(
            jax.ShapeDtypeStruct((3 * examples, row_width), jnp.bfloat16),
            jax.ShapeDtypeStruct((3 * examples, col_width), jnp.bfloat16),
            jax.ShapeDtypeStruct((examples, count), f32),
        ),
        in_specs=[pl.BlockSpec(memory_space=pltpu.SMEM)] + [pl.BlockSpec(memory_space=pltpu.VMEM)] * 2,
    )(at, both, query_side)
    total = 2 * half * half
    scores = scores / jnp.sqrt(f32(total))
    for axis, size in (("fsdp", n), ("solve", m)):
        bit = 1
        while bit < size:
            scores = scores + swap(scores, axis, size, bit)
            bit *= 2
    block = 128
    steps = row_width // block
    ends = [0, steps // 2, steps]
    new_gram = None
    for a, b in zip(ends[:-1], ends[1:]):
        in_specs = [
            pl.BlockSpec((block, col_width), functools.partial(lambda z, i: (z + i, 0), a)),
            pl.BlockSpec((3 * examples, block), functools.partial(lambda z, i: (0, z + i), a)),
            pl.BlockSpec((3 * examples, col_width), lambda i: (0, 0)),
        ]
        operands = [gram, left, right]
        if new_gram is not None:
            in_specs.append(pl.BlockSpec(memory_space=pl.ANY))
            operands.append(new_gram)
        new_gram = pl.pallas_call(
            functools.partial(gram_kernel, 1.0 / examples),
            out_shape=jax.ShapeDtypeStruct(gram.shape, f32),
            grid=(b - a,),
            in_specs=in_specs,
            out_specs=pl.BlockSpec((block, col_width), functools.partial(lambda z, i: (z + i, 0), a)),
            input_output_aliases={} if new_gram is None else {3: 0},
        )(*operands)
    return (new_gram, whitened, scores)


def solution(mesh):
    in_specs = (
        P("fsdp", "solve"),
        P("fsdp", "solve"),
        P("fsdp", "solve"),
        P("fsdp", "solve"),
        P("solve", "fsdp"),
        P("solve", None),
        P("solve", None),
        P("fsdp"),
        P("fsdp", "solve"),
        P("fsdp", "solve"),
        P("solve", "fsdp"),
    )
    out_specs = (P("fsdp", "solve"), P(("fsdp", "solve"), None), P())

    def body(*args):
        return local(mesh.shape["fsdp"], mesh.shape["solve"], *args)

    return jax.shard_map(body, mesh=mesh, in_specs=in_specs, out_specs=out_specs, check_vma=False)
```

```python
import functools

import jax
import jax.numpy as jnp
from jax import lax
from jax.experimental import pallas as pl
from jax.experimental.pallas import tpu as pltpu
from jax.sharding import PartitionSpec as P


SEQ_LEN = 256
TILE = 256


def tokens_kernel(count, gates, chained, idx, *refs):
    del idx
    cots, refs = refs[:count], refs[count:]
    weights, refs = refs[:count], refs[count:]
    gate_refs, refs = refs[:gates], refs[gates:]
    if chained:
        start, refs = refs[0], refs[1:]
    proj, out = refs

    @pl.when(pl.program_id(0) == 0)
    def _():
        out[...] = start[...] if chained else jnp.zeros_like(out)

    grad = None
    for cot, weight in zip(cots, weights):
        term = lax.dot_general(
            cot[...], weight[...], (((1,), (1,)), ((), ())), preferred_element_type=jnp.float32
        )
        grad = term if grad is None else grad + term
    gate = gate_refs[0][...].astype(jnp.float32)
    for other in gate_refs[1:]:
        gate = gate + other[...].astype(jnp.float32)
    smooth = gate * jax.nn.sigmoid(gate)
    grad_up = (grad * smooth).astype(jnp.bfloat16)
    out[...] += jnp.dot(grad_up, proj[...], preferred_element_type=jnp.float32)


def tokens(idx, cot, weights, gate_parts, start, proj, first, tiles):
    count = len(weights)
    rows = cot.shape[0]
    width = weights[0][0].shape[1]
    in_specs = [
        pl.BlockSpec(
            (rows, width), functools.partial(lambda k, i, ix: (0, ix[k]), k), pipeline_mode=pl.Buffered(1)
        )
        for k in range(count)
    ]
    for _, shift in weights:
        in_specs.append(pl.BlockSpec((TILE, width), functools.partial(lambda a, i, ix: (a + i, 0), shift)))
    for _, shift in gate_parts:
        in_specs.append(pl.BlockSpec((rows, TILE), functools.partial(lambda a, i, ix: (0, a + i), shift)))
    operands = [cot] * count + [part for part, _ in weights] + [part for part, _ in gate_parts]
    whole = pl.BlockSpec((rows, proj.shape[1]), lambda i, ix: (0, 0))
    if start is not None:
        in_specs.append(whole)
        operands.append(start)
    in_specs.append(pl.BlockSpec((TILE, proj.shape[1]), lambda i, ix: (first + i, 0)))
    operands.append(proj)
    return pl.pallas_call(
        functools.partial(tokens_kernel, count, len(gate_parts), start is not None),
        out_shape=jax.ShapeDtypeStruct((rows, proj.shape[1]), jnp.float32),
        grid_spec=pltpu.PrefetchScalarGridSpec(
            num_scalar_prefetch=1,
            grid=(tiles,),
            in_specs=in_specs,
            out_specs=whole,
        ),
        compiler_params=pltpu.CompilerParams(dimension_semantics=("arbitrary",)),
        cost_estimate=pl.CostEstimate(
            flops=2 * rows * TILE * tiles * (count * width + 256),
            bytes_accessed=TILE * tiles * (count * width + 2 * rows) * 2 + rows * count * width * 2,
            transcendentals=rows * TILE * tiles,
        ),
    )(idx, *operands)


def features_kernel(examples, seqs, count, idx, both, other, left_out, right_out, scores):
    f32 = jnp.float32
    shape = (examples, both.shape[0])
    pick = lax.broadcasted_iota(jnp.int32, shape, 1)
    row = lax.broadcasted_iota(jnp.int32, shape, 0)
    up = jnp.zeros(shape, f32)
    down = jnp.zeros(shape, f32)
    for i in range(examples // seqs):
        for e in range(seqs):
            here = row == seqs * i + e
            up = jnp.where((pick == 2 * seqs * i + e) & here, 1.0, up)
            down = jnp.where((pick == 2 * seqs * i + seqs + e) & here, 1.0, down)

    def split(x):
        high = x.astype(jnp.bfloat16)
        return high, (x - high.astype(f32)).astype(jnp.bfloat16)

    def part(offset, width):
        size = both.shape[1]
        is_up = offset >= size
        at = pl.multiple_of(offset - jnp.where(is_up, size, 0), 128)
        high, low = split(both[:, pl.ds(at, width)])
        sel = jnp.where(is_up, up, down).astype(jnp.bfloat16)
        return jnp.dot(sel, high, preferred_element_type=f32) + jnp.dot(sel, low, preferred_element_type=f32)

    high, low = split(part(idx[0], left_out.shape[1]))
    left_out[...] = jnp.concatenate([high, low, high], axis=0)
    right = part(idx[1], right_out.shape[1])
    high, low = split(right)
    right_out[...] = jnp.concatenate([high, high, low], axis=0)
    product = lax.dot_general(
        right,
        other[...],
        (((1,), (1,)), ((), ())),
        precision=lax.Precision.HIGHEST,
        preferred_element_type=f32,
    )
    scores[...] = product / jnp.sqrt(f32(count))


def gram_kernel(scale, gram, left, right, *refs):
    out = refs[-1]
    term = lax.dot_general(
        left[...], right[...], (((0,), (0,)), ((), ())), preferred_element_type=jnp.float32
    )
    out[...] = gram[...] + term * scale


def local(
    n,
    m,
    inputs,
    cotangent,
    gate_pre,
    up_pre,
    down_weight,
    proj_model,
    proj_hidden,
    lengths,
    gram,
    inverse_factor,
    queries,
):
    top = lax.Precision.HIGHEST
    f32 = jnp.float32
    f = lax.axis_index("fsdp")
    s = lax.axis_index("solve")
    rows = inputs.shape[0]
    local_seqs = lengths.shape[0]
    half = proj_model.shape[1] // 2
    h = n // 2
    chips = n // 2
    side = f // h

    def swap(x, axis, size, bit):
        return lax.ppermute(x, axis, [(i, i ^ bit) for i in range(size)])

    def total(x, axis, size):
        bit = 1
        while bit < size:
            if 2 * bit < size:
                one, two, both = (swap(x, axis, size, b) for b in (bit, 2 * bit, 3 * bit))
                x = (x + one) + (two + both)
            else:
                x = x + swap(x, axis, size, bit)
            bit *= 4
        return x

    mirror_of = [(chips - 1 - i // 2) * 2 + i % 2 for i in range(n)]

    def mirror(x, keep=lambda chip: True):
        pairs = [(i, mirror_of[i]) for i in range(n) if keep(i // 2)]
        return lax.ppermute(x, "fsdp", pairs)

    def inner(chip):
        return chips // 4 <= chip < chips - chips // 4

    tiles = gate_pre.shape[1] // TILE
    blocks = {0: down_weight}
    step = 2
    while step < h:
        blocks.update({k ^ step: swap(v, "fsdp", n, step) for k, v in list(blocks.items())})
        step *= 2
    gate_inner = mirror(gate_pre, inner)
    cot_full = lax.all_gather(cotangent, "solve", axis=1, tiled=True)
    part = rows // m
    near = cot_full.shape[1] // 2
    quarter = lax.dynamic_slice(cot_full, (s * part, (1 - side) * near), (part, near))
    quarter = mirror(quarter)
    cot_far = lax.all_gather(quarter, "solve", axis=0, tiled=True)
    sibling = swap(down_weight, "fsdp", n, 1)
    blocks.update({k ^ 1: swap(v, "fsdp", n, 1) for k, v in list(blocks.items()) if k})
    blocks[1] = sibling
    order = sorted(blocks)
    weights = [blocks[k] for k in order]
    share = max(1, tiles // 7)
    cuts = [0, tiles - 3 * share, tiles - share, tiles]
    chunks = []
    for j, (a, b) in enumerate(zip(cuts[:-1], cuts[1:])):
        gate_outer, _ = lax.optimization_barrier((gate_pre[:, a * TILE : b * TILE], quarter))
        gate_outer = mirror(gate_outer, lambda chip: not inner(chip))
        chunks.append((j, a, b, gate_outer))

    gate = gate_pre.astype(f32)
    hidden = (gate * jax.nn.sigmoid(gate) * up_pre.astype(f32)).astype(jnp.bfloat16)
    early = jnp.concatenate(
        [
            jnp.dot(hidden, proj_hidden[:, :half], preferred_element_type=f32),
            jnp.dot(cotangent, proj_model[:, :half], preferred_element_type=f32),
            jnp.dot(inputs, proj_model[:, half:], preferred_element_type=f32),
        ],
        axis=1,
    )
    early = total(early, "solve", m)

    query_block = lax.all_gather(queries.astype(jnp.bfloat16), "fsdp", axis=1, tiled=True)
    partial = jnp.dot(inverse_factor, query_block.astype(f32), precision=lax.Precision.HIGH)
    whitened = partial
    bit = m // 2
    while bit:
        size = whitened.shape[0] // 2
        mine = s // bit % 2
        moved = swap(lax.dynamic_slice_in_dim(whitened, (1 - mine) * size, size, 0), "solve", m, bit)
        whitened = lax.dynamic_slice_in_dim(whitened, mine * size, size, 0) + moved
        bit //= 2
    whitened_rows = whitened
    bit = 1
    while bit < m:
        mine = s // bit % 2
        moved = swap(whitened_rows, "solve", m, bit)
        whitened_rows = jnp.where(
            mine == 0,
            jnp.concatenate([whitened_rows, moved], axis=0),
            jnp.concatenate([moved, whitened_rows], axis=0),
        )
        bit *= 2
    query_side = lax.dot_general(whitened_rows, inverse_factor, (((0,), (0,)), ((), ())), precision=lax.Precision.HIGH)

    own_idx = jnp.stack([f ^ k for k in order]).astype(jnp.int32)
    far_idx = own_idx - side * h
    own = tokens(
        own_idx, cot_full, [(v, 0) for v in weights], [(gate_pre, 0)], None, proj_hidden, 0, tiles
    )
    token_index = lax.broadcasted_iota(jnp.int32, (rows, 1), 0)
    slots = lax.broadcasted_iota(jnp.int32, (1, local_seqs), 1)
    length_of = jnp.sum(
        jnp.where(token_index // SEQ_LEN == slots, lengths[None, :], 0), axis=1, keepdims=True
    )
    weight_of = jnp.where(
        token_index % SEQ_LEN < length_of, 1.0 / jnp.sqrt(length_of.astype(f32)), 0.0
    )
    in_down = early[:, :half]
    out_down = early[:, half : 2 * half] * weight_of
    in_up = early[:, 2 * half :] * weight_of
    in_up_far = mirror(in_up.astype(jnp.bfloat16)).astype(f32)

    def pair(outs, ins):
        shape = (local_seqs, SEQ_LEN, half)
        feat = jnp.einsum("eto,eti->eoi", outs.reshape(shape), ins.reshape(shape), precision=top)
        return feat.reshape(local_seqs, half * half)

    down = pair(out_down, in_down)
    up_own = pair(own[:, half:], in_up)

    far = None
    for j, a, b, gate_outer in chunks:
        if j == len(chunks) - 1:
            far_idx, query_side = lax.optimization_barrier((far_idx, query_side))
        gates = [(gate_inner, a), (gate_outer, 0)]
        far = tokens(far_idx, cot_far, [(v, a) for v in weights], gates, far, proj_hidden, a, b - a)
    up_far = pair(far[:, half:], in_up_far)
    up = up_own + mirror(up_far)
    up = total(up, "solve", m)
    both = lax.all_gather(jnp.concatenate([up, down], axis=0), "fsdp", axis=0, tiled=True)

    examples = n * local_seqs
    row_width = gram.shape[0]
    col_width = gram.shape[1]
    count = queries.shape[1] * n
    at = jnp.stack([f * row_width, s * col_width]).astype(jnp.int32)
    left, right, scores = pl.pallas_call(
        functools.partial(features_kernel, examples, local_seqs, 2 * half * half),
        out_shape=(
            jax.ShapeDtypeStruct((3 * examples, row_width), jnp.bfloat16),
            jax.ShapeDtypeStruct((3 * examples, col_width), jnp.bfloat16),
            jax.ShapeDtypeStruct((examples, count), f32),
        ),
        in_specs=[pl.BlockSpec(memory_space=pltpu.SMEM)] + [pl.BlockSpec(memory_space=pltpu.VMEM)] * 2,
    )(at, both, query_side)
    scores = total(scores, "fsdp", n)
    scores = total(scores, "solve", m)
    block = 128
    steps = row_width // block
    ends = [0, steps // 2, steps]
    new_gram = None
    for a, b in zip(ends[:-1], ends[1:]):
        in_specs = [
            pl.BlockSpec((block, col_width), functools.partial(lambda z, i: (z + i, 0), a)),
            pl.BlockSpec((3 * examples, block), functools.partial(lambda z, i: (0, z + i), a)),
            pl.BlockSpec((3 * examples, col_width), lambda i: (0, 0)),
        ]
        operands = [gram, left, right]
        if new_gram is not None:
            in_specs.append(pl.BlockSpec(memory_space=pl.ANY))
            operands.append(new_gram)
        new_gram = pl.pallas_call(
            functools.partial(gram_kernel, 1.0 / examples),
            out_shape=jax.ShapeDtypeStruct(gram.shape, f32),
            grid=(b - a,),
            in_specs=in_specs,
            out_specs=pl.BlockSpec((block, col_width), functools.partial(lambda z, i: (z + i, 0), a)),
            input_output_aliases={} if new_gram is None else {3: 0},
        )(*operands)
    return (new_gram, whitened, scores)


def solution(mesh):
    in_specs = (
        P("fsdp", "solve"),
        P("fsdp", "solve"),
        P("fsdp", "solve"),
        P("fsdp", "solve"),
        P("solve", "fsdp"),
        P("solve", None),
        P("solve", None),
        P("fsdp"),
        P("fsdp", "solve"),
        P("fsdp", "solve"),
        P("solve", "fsdp"),
    )
    out_specs = (P("fsdp", "solve"), P(("fsdp", "solve"), None), P())

    def body(*args):
        return local(mesh.shape["fsdp"], mesh.shape["solve"], *args)

    return jax.shard_map(body, mesh=mesh, in_specs=in_specs, out_specs=out_specs, check_vma=False)
```

```python
import functools

import jax
import jax.numpy as jnp
from jax import lax
from jax.experimental import pallas as pl
from jax.experimental.pallas import tpu as pltpu
from jax.sharding import PartitionSpec as P


SEQ_LEN = 256
TILE = 256


def tokens_kernel(count, gates, chained, idx, *refs):
    del idx
    cots, refs = refs[:count], refs[count:]
    weights, refs = refs[:count], refs[count:]
    gate_refs, refs = refs[:gates], refs[gates:]
    if chained:
        start, refs = refs[0], refs[1:]
    proj, out = refs

    @pl.when(pl.program_id(0) == 0)
    def _():
        out[...] = start[...] if chained else jnp.zeros_like(out)

    grad = None
    for cot, weight in zip(cots, weights):
        term = lax.dot_general(
            cot[...], weight[...], (((1,), (1,)), ((), ())), preferred_element_type=jnp.float32
        )
        grad = term if grad is None else grad + term
    gate = gate_refs[0][...].astype(jnp.float32)
    for other in gate_refs[1:]:
        gate = gate + other[...].astype(jnp.float32)
    smooth = gate * jax.nn.sigmoid(gate)
    grad_up = (grad * smooth).astype(jnp.bfloat16)
    out[...] += jnp.dot(grad_up, proj[...], preferred_element_type=jnp.float32)


def tokens(idx, cot, weights, gate_parts, start, proj, first, tiles):
    count = len(weights)
    rows = cot.shape[0]
    width = weights[0][0].shape[1]
    in_specs = [
        pl.BlockSpec(
            (rows, width), functools.partial(lambda k, i, ix: (0, ix[k]), k), pipeline_mode=pl.Buffered(1)
        )
        for k in range(count)
    ]
    for _, shift in weights:
        in_specs.append(pl.BlockSpec((TILE, width), functools.partial(lambda a, i, ix: (a + i, 0), shift)))
    for _, shift in gate_parts:
        in_specs.append(pl.BlockSpec((rows, TILE), functools.partial(lambda a, i, ix: (0, a + i), shift)))
    operands = [cot] * count + [part for part, _ in weights] + [part for part, _ in gate_parts]
    whole = pl.BlockSpec((rows, proj.shape[1]), lambda i, ix: (0, 0))
    if start is not None:
        in_specs.append(whole)
        operands.append(start)
    in_specs.append(pl.BlockSpec((TILE, proj.shape[1]), lambda i, ix: (first + i, 0)))
    operands.append(proj)
    return pl.pallas_call(
        functools.partial(tokens_kernel, count, len(gate_parts), start is not None),
        out_shape=jax.ShapeDtypeStruct((rows, proj.shape[1]), jnp.float32),
        grid_spec=pltpu.PrefetchScalarGridSpec(
            num_scalar_prefetch=1,
            grid=(tiles,),
            in_specs=in_specs,
            out_specs=whole,
        ),
        compiler_params=pltpu.CompilerParams(dimension_semantics=("arbitrary",)),
        cost_estimate=pl.CostEstimate(
            flops=2 * rows * TILE * tiles * (count * width + 256),
            bytes_accessed=TILE * tiles * (count * width + 2 * rows) * 2 + rows * count * width * 2,
            transcendentals=rows * TILE * tiles,
        ),
    )(idx, *operands)


def grad_kernel(count, idx, *refs):
    del idx
    out = refs[-1]
    grad = None
    for cot, weight in zip(refs[:count], refs[count : 2 * count]):
        term = lax.dot_general(
            cot[...], weight[...], (((1,), (1,)), ((), ())), preferred_element_type=jnp.float32
        )
        grad = term if grad is None else grad + term
    out[...] = grad


def gradient(idx, cot, weights):
    count = len(weights)
    rows = cot.shape[0]
    units, width = weights[0].shape
    in_specs = [
        pl.BlockSpec(
            (rows, width), functools.partial(lambda k, i, ix: (0, ix[k]), k), pipeline_mode=pl.Buffered(1)
        )
        for k in range(count)
    ]
    in_specs += [pl.BlockSpec((TILE, width), lambda i, ix: (i, 0))] * count
    return pl.pallas_call(
        functools.partial(grad_kernel, count),
        out_shape=jax.ShapeDtypeStruct((rows, units), jnp.float32),
        grid_spec=pltpu.PrefetchScalarGridSpec(
            num_scalar_prefetch=1,
            grid=(units // TILE,),
            in_specs=in_specs,
            out_specs=pl.BlockSpec((rows, TILE), lambda i, ix: (0, i)),
        ),
        compiler_params=pltpu.CompilerParams(dimension_semantics=("arbitrary",)),
        cost_estimate=pl.CostEstimate(
            flops=2 * rows * units * count * width,
            bytes_accessed=units * count * width * 2 + rows * count * width * 2 + rows * units * 4,
            transcendentals=0,
        ),
    )(idx, *([cot] * count), *weights)


def features_kernel(examples, seqs, count, idx, both, other, left_out, right_out, scores):
    f32 = jnp.float32
    shape = (examples, both.shape[0])
    pick = lax.broadcasted_iota(jnp.int32, shape, 1)
    row = lax.broadcasted_iota(jnp.int32, shape, 0)
    up = jnp.zeros(shape, f32)
    down = jnp.zeros(shape, f32)
    for i in range(examples // seqs):
        for e in range(seqs):
            here = row == seqs * i + e
            up = jnp.where((pick == 2 * seqs * i + e) & here, 1.0, up)
            down = jnp.where((pick == 2 * seqs * i + seqs + e) & here, 1.0, down)

    def split(x):
        high = x.astype(jnp.bfloat16)
        return high, (x - high.astype(f32)).astype(jnp.bfloat16)

    def part(offset, width):
        size = both.shape[1]
        is_up = offset >= size
        at = pl.multiple_of(offset - jnp.where(is_up, size, 0), 128)
        high, low = split(both[:, pl.ds(at, width)])
        sel = jnp.where(is_up, up, down).astype(jnp.bfloat16)
        return jnp.dot(sel, high, preferred_element_type=f32) + jnp.dot(sel, low, preferred_element_type=f32)

    high, low = split(part(idx[0], left_out.shape[1]))
    left_out[...] = jnp.concatenate([high, low, high], axis=0)
    right = part(idx[1], right_out.shape[1])
    high, low = split(right)
    right_out[...] = jnp.concatenate([high, high, low], axis=0)
    product = lax.dot_general(
        right,
        other[...],
        (((1,), (1,)), ((), ())),
        precision=lax.Precision.HIGHEST,
        preferred_element_type=f32,
    )
    scores[...] = product / jnp.sqrt(f32(count))


def gram_kernel(scale, gram, left, right, *refs):
    out = refs[-1]
    term = lax.dot_general(
        left[...], right[...], (((0,), (0,)), ((), ())), preferred_element_type=jnp.float32
    )
    out[...] = gram[...] + term * scale


def local(
    n,
    m,
    inputs,
    cotangent,
    gate_pre,
    up_pre,
    down_weight,
    proj_model,
    proj_hidden,
    lengths,
    gram,
    inverse_factor,
    queries,
):
    top = lax.Precision.HIGHEST
    f32 = jnp.float32
    f = lax.axis_index("fsdp")
    s = lax.axis_index("solve")
    rows = inputs.shape[0]
    local_seqs = lengths.shape[0]
    half = proj_model.shape[1] // 2
    h = n // 2
    chips = n // 2
    side = f // h

    def swap(x, axis, size, bit):
        return lax.ppermute(x, axis, [(i, i ^ bit) for i in range(size)])

    def total(x, axis, size):
        bit = 1
        while bit < size:
            if 2 * bit < size:
                one, two, both = (swap(x, axis, size, b) for b in (bit, 2 * bit, 3 * bit))
                x = (x + one) + (two + both)
            else:
                x = x + swap(x, axis, size, bit)
            bit *= 4
        return x

    mirror_of = [(chips - 1 - i // 2) * 2 + i % 2 for i in range(n)]

    def mirror(x, keep=lambda chip: True):
        pairs = [(i, mirror_of[i]) for i in range(n) if keep(i // 2)]
        return lax.ppermute(x, "fsdp", pairs)

    def inner(chip):
        return chips // 4 <= chip < chips - chips // 4

    tiles = gate_pre.shape[1] // TILE
    blocks = {0: down_weight}
    step = 2
    while step < h:
        blocks.update({k ^ step: swap(v, "fsdp", n, step) for k, v in list(blocks.items())})
        step *= 2
    gate_inner = mirror(gate_pre, inner)
    cot_full = lax.all_gather(cotangent, "solve", axis=1, tiled=True)
    part = rows // m
    near = cot_full.shape[1] // 2
    quarter = lax.dynamic_slice(cot_full, (s * part, (1 - side) * near), (part, near))
    quarter = mirror(quarter)
    cot_far = lax.all_gather(quarter, "solve", axis=0, tiled=True)
    sibling = swap(down_weight, "fsdp", n, 1)
    blocks.update({k ^ 1: swap(v, "fsdp", n, 1) for k, v in list(blocks.items()) if k})
    blocks[1] = sibling
    order = sorted(blocks)
    weights = [blocks[k] for k in order]
    share = max(1, tiles // 7)
    cuts = [0, tiles - 3 * share, tiles - share, tiles]
    chunks = []
    for j, (a, b) in enumerate(zip(cuts[:-1], cuts[1:])):
        gate_outer, _ = lax.optimization_barrier((gate_pre[:, a * TILE : b * TILE], quarter))
        gate_outer = mirror(gate_outer, lambda chip: not inner(chip))
        chunks.append((j, a, b, gate_outer))

    gate = gate_pre.astype(f32)
    hidden = (gate * jax.nn.sigmoid(gate) * up_pre.astype(f32)).astype(jnp.bfloat16)
    early = jnp.concatenate(
        [
            jnp.dot(hidden, proj_hidden[:, :half], preferred_element_type=f32),
            jnp.dot(cotangent, proj_model[:, :half], preferred_element_type=f32),
            jnp.dot(inputs, proj_model[:, half:], preferred_element_type=f32),
        ],
        axis=1,
    )
    early = total(early, "solve", m)

    query_block = lax.all_gather(queries.astype(jnp.bfloat16), "fsdp", axis=1, tiled=True)
    partial = jnp.dot(inverse_factor, query_block.astype(f32), precision=lax.Precision.HIGH)
    whitened = partial
    bit = m // 2
    while bit:
        size = whitened.shape[0] // 2
        mine = s // bit % 2
        moved = swap(lax.dynamic_slice_in_dim(whitened, (1 - mine) * size, size, 0), "solve", m, bit)
        whitened = lax.dynamic_slice_in_dim(whitened, mine * size, size, 0) + moved
        bit //= 2
    whitened_rows = whitened
    bit = 1
    while bit < m:
        mine = s // bit % 2
        moved = swap(whitened_rows, "solve", m, bit)
        whitened_rows = jnp.where(
            mine == 0,
            jnp.concatenate([whitened_rows, moved], axis=0),
            jnp.concatenate([moved, whitened_rows], axis=0),
        )
        bit *= 2
    query_side = lax.dot_general(whitened_rows, inverse_factor, (((0,), (0,)), ((), ())), precision=lax.Precision.HIGH)

    own_idx = jnp.stack([f ^ k for k in order]).astype(jnp.int32)
    far_idx = own_idx - side * h
    own_idx, query_side = lax.optimization_barrier((own_idx, query_side))
    own = tokens(
        own_idx, cot_full, [(v, 0) for v in weights], [(gate_pre, 0)], None, proj_hidden, 0, tiles
    )
    token_index = lax.broadcasted_iota(jnp.int32, (rows, 1), 0)
    slots = lax.broadcasted_iota(jnp.int32, (1, local_seqs), 1)
    length_of = jnp.sum(
        jnp.where(token_index // SEQ_LEN == slots, lengths[None, :], 0), axis=1, keepdims=True
    )
    weight_of = jnp.where(
        token_index % SEQ_LEN < length_of, 1.0 / jnp.sqrt(length_of.astype(f32)), 0.0
    )
    in_down = early[:, :half]
    out_down = early[:, half : 2 * half] * weight_of
    in_up = early[:, 2 * half :] * weight_of
    in_up_far = mirror(in_up.astype(jnp.bfloat16)).astype(f32)

    def pair(outs, ins):
        shape = (local_seqs, SEQ_LEN, half)
        feat = jnp.einsum("eto,eti->eoi", outs.reshape(shape), ins.reshape(shape), precision=top)
        return feat.reshape(local_seqs, half * half)

    down = pair(out_down, in_down)
    up_own = pair(own[:, half:], in_up)

    grad = gradient(far_idx, cot_far, weights)
    far = None
    for j, a, b, gate_outer in chunks:
        if far is not None:
            gate_outer, far = lax.optimization_barrier((gate_outer, far))
        units = slice(a * TILE, b * TILE)
        gate = gate_inner[:, units].astype(f32) + gate_outer.astype(f32)
        grad_up = (grad[:, units] * (gate * jax.nn.sigmoid(gate))).astype(jnp.bfloat16)
        term = jnp.dot(grad_up, proj_hidden[units, half:], preferred_element_type=f32)
        far = term if far is None else far + term
    up_far = pair(far, in_up_far)
    up = up_own + mirror(up_far)
    up = total(up, "solve", m)
    both = lax.all_gather(jnp.concatenate([up, down], axis=0), "fsdp", axis=0, tiled=True)

    examples = n * local_seqs
    row_width = gram.shape[0]
    col_width = gram.shape[1]
    count = queries.shape[1] * n
    at = jnp.stack([f * row_width, s * col_width]).astype(jnp.int32)
    left, right, scores = pl.pallas_call(
        functools.partial(features_kernel, examples, local_seqs, 2 * half * half),
        out_shape=(
            jax.ShapeDtypeStruct((3 * examples, row_width), jnp.bfloat16),
            jax.ShapeDtypeStruct((3 * examples, col_width), jnp.bfloat16),
            jax.ShapeDtypeStruct((examples, count), f32),
        ),
        in_specs=[pl.BlockSpec(memory_space=pltpu.SMEM)] + [pl.BlockSpec(memory_space=pltpu.VMEM)] * 2,
    )(at, both, query_side)
    scores = total(scores, "fsdp", n)
    scores = total(scores, "solve", m)
    block = 128
    steps = row_width // block
    ends = [0, steps // 2, steps]
    new_gram = None
    for a, b in zip(ends[:-1], ends[1:]):
        in_specs = [
            pl.BlockSpec((block, col_width), functools.partial(lambda z, i: (z + i, 0), a)),
            pl.BlockSpec((3 * examples, block), functools.partial(lambda z, i: (0, z + i), a)),
            pl.BlockSpec((3 * examples, col_width), lambda i: (0, 0)),
        ]
        operands = [gram, left, right]
        if new_gram is not None:
            in_specs.append(pl.BlockSpec(memory_space=pl.ANY))
            operands.append(new_gram)
        new_gram = pl.pallas_call(
            functools.partial(gram_kernel, 1.0 / examples),
            out_shape=jax.ShapeDtypeStruct(gram.shape, f32),
            grid=(b - a,),
            in_specs=in_specs,
            out_specs=pl.BlockSpec((block, col_width), functools.partial(lambda z, i: (z + i, 0), a)),
            input_output_aliases={} if new_gram is None else {3: 0},
        )(*operands)
    return (new_gram, whitened, scores)


def solution(mesh):
    in_specs = (
        P("fsdp", "solve"),
        P("fsdp", "solve"),
        P("fsdp", "solve"),
        P("fsdp", "solve"),
        P("solve", "fsdp"),
        P("solve", None),
        P("solve", None),
        P("fsdp"),
        P("fsdp", "solve"),
        P("fsdp", "solve"),
        P("solve", "fsdp"),
    )
    out_specs = (P("fsdp", "solve"), P(("fsdp", "solve"), None), P())

    def body(*args):
        return local(mesh.shape["fsdp"], mesh.shape["solve"], *args)

    return jax.shard_map(body, mesh=mesh, in_specs=in_specs, out_specs=out_specs, check_vma=False)
```

```python
import functools
import math

import jax
import jax.numpy as jnp
from jax import lax
from jax.experimental import pallas as pl
from jax.experimental.pallas import tpu as pltpu
from jax.sharding import PartitionSpec as P


SEQ_LEN = 256
TILE = 256


def tokens_kernel(count, gates, chained, idx, *refs):
    del idx
    cots, refs = refs[:count], refs[count:]
    weights, refs = refs[:count], refs[count:]
    gate_refs, refs = refs[:gates], refs[gates:]
    if chained:
        start, refs = refs[0], refs[1:]
    proj, out = refs

    @pl.when(pl.program_id(0) == 0)
    def _():
        out[...] = start[...] if chained else jnp.zeros_like(out)

    grad = None
    for cot, weight in zip(cots, weights):
        term = lax.dot_general(
            cot[...], weight[...], (((1,), (1,)), ((), ())), preferred_element_type=jnp.float32
        )
        grad = term if grad is None else grad + term
    gate = gate_refs[0][...].astype(jnp.float32)
    for other in gate_refs[1:]:
        gate = gate + other[...].astype(jnp.float32)
    smooth = gate * jax.nn.sigmoid(gate)
    grad_up = (grad * smooth).astype(jnp.bfloat16)
    out[...] += jnp.dot(grad_up, proj[...], preferred_element_type=jnp.float32)


def tokens(idx, cot, weights, gate_parts, start, proj, first, tiles):
    count = len(weights)
    rows = cot.shape[0]
    width = weights[0][0].shape[1]
    in_specs = [
        pl.BlockSpec(
            (rows, width), functools.partial(lambda k, i, ix: (0, ix[k]), k), pipeline_mode=pl.Buffered(1)
        )
        for k in range(count)
    ]
    for _, shift in weights:
        in_specs.append(pl.BlockSpec((TILE, width), functools.partial(lambda a, i, ix: (a + i, 0), shift)))
    for _, shift in gate_parts:
        in_specs.append(pl.BlockSpec((rows, TILE), functools.partial(lambda a, i, ix: (0, a + i), shift)))
    operands = [cot] * count + [part for part, _ in weights] + [part for part, _ in gate_parts]
    whole = pl.BlockSpec((rows, proj.shape[1]), lambda i, ix: (0, 0))
    if start is not None:
        in_specs.append(whole)
        operands.append(start)
    in_specs.append(pl.BlockSpec((TILE, proj.shape[1]), lambda i, ix: (first + i, 0)))
    operands.append(proj)
    return pl.pallas_call(
        functools.partial(tokens_kernel, count, len(gate_parts), start is not None),
        out_shape=jax.ShapeDtypeStruct((rows, proj.shape[1]), jnp.float32),
        grid_spec=pltpu.PrefetchScalarGridSpec(
            num_scalar_prefetch=1,
            grid=(tiles,),
            in_specs=in_specs,
            out_specs=whole,
        ),
        compiler_params=pltpu.CompilerParams(dimension_semantics=("arbitrary",)),
        cost_estimate=pl.CostEstimate(
            flops=2 * rows * TILE * tiles * (count * width + 256),
            bytes_accessed=TILE * tiles * (count * width + 2 * rows) * 2 + rows * count * width * 2,
            transcendentals=rows * TILE * tiles,
        ),
    )(idx, *operands)


def grad_kernel(count, idx, *refs):
    del idx
    out = refs[-1]
    grad = None
    for cot, weight in zip(refs[:count], refs[count : 2 * count]):
        term = lax.dot_general(
            cot[...], weight[...], (((1,), (1,)), ((), ())), preferred_element_type=jnp.float32
        )
        grad = term if grad is None else grad + term
    out[...] = grad


def gradient(idx, cot, weights):
    count = len(weights)
    rows = cot.shape[0]
    units, width = weights[0].shape
    in_specs = [
        pl.BlockSpec(
            (rows, width), functools.partial(lambda k, i, ix: (0, ix[k]), k), pipeline_mode=pl.Buffered(1)
        )
        for k in range(count)
    ]
    in_specs += [pl.BlockSpec((TILE, width), lambda i, ix: (i, 0))] * count
    return pl.pallas_call(
        functools.partial(grad_kernel, count),
        out_shape=jax.ShapeDtypeStruct((rows, units), jnp.float32),
        grid_spec=pltpu.PrefetchScalarGridSpec(
            num_scalar_prefetch=1,
            grid=(units // TILE,),
            in_specs=in_specs,
            out_specs=pl.BlockSpec((rows, TILE), lambda i, ix: (0, i)),
        ),
        compiler_params=pltpu.CompilerParams(dimension_semantics=("arbitrary",)),
        cost_estimate=pl.CostEstimate(
            flops=2 * rows * units * count * width,
            bytes_accessed=units * count * width * 2 + rows * count * width * 2 + rows * units * 4,
            transcendentals=0,
        ),
    )(idx, *([cot] * count), *weights)


def split(x):
    high = x.astype(jnp.bfloat16)
    return high, (x - high.astype(jnp.float32)).astype(jnp.bfloat16)


def features_kernel(scale, idx, both, pick_left, pick_right, high_side, low_side, left_out, right_out, scores):
    f32 = jnp.float32

    def part(offset, width, pick):
        at = pl.multiple_of(offset, 128)
        high, low = split(both[:, pl.ds(at, width)])
        return jnp.dot(pick, high, preferred_element_type=f32) + jnp.dot(pick, low, preferred_element_type=f32)

    def against(x, side):
        return lax.dot_general(x, side, (((1,), (1,)), ((), ())), preferred_element_type=f32)

    high, low = split(part(idx[0], left_out.shape[1], pick_left[...]))
    left_out[...] = jnp.concatenate([high, low, high], axis=0)
    high, low = split(part(idx[1], right_out.shape[1], pick_right[...]))
    right_out[...] = jnp.concatenate([high, high, low], axis=0)
    product = against(high, high_side[...]) + (against(low, high_side[...]) + against(high, low_side[...]))
    scores[...] = product * scale


def gram_kernel(scale, gram, left, right, *refs):
    out = refs[-1]
    term = lax.dot_general(
        left[...], right[...], (((0,), (0,)), ((), ())), preferred_element_type=jnp.float32
    )
    out[...] = gram[...] + term * scale


def local(
    n,
    m,
    inputs,
    cotangent,
    gate_pre,
    up_pre,
    down_weight,
    proj_model,
    proj_hidden,
    lengths,
    gram,
    inverse_factor,
    queries,
):
    top = lax.Precision.HIGHEST
    f32 = jnp.float32
    f = lax.axis_index("fsdp")
    s = lax.axis_index("solve")
    rows = inputs.shape[0]
    local_seqs = lengths.shape[0]
    half = proj_model.shape[1] // 2
    h = n // 2
    chips = n // 2
    side = f // h

    def swap(x, axis, size, bit):
        return lax.ppermute(x, axis, [(i, i ^ bit) for i in range(size)])

    def total(x, axis, size, bit=1):
        while bit < size:
            if 2 * bit < size:
                one, two, both = (swap(x, axis, size, b) for b in (bit, 2 * bit, 3 * bit))
                x = (x + one) + (two + both)
            else:
                x = x + swap(x, axis, size, bit)
            bit *= 4
        return x

    mirror_of = [(chips - 1 - i // 2) * 2 + i % 2 for i in range(n)]

    def mirror(x, keep=lambda chip: True):
        pairs = [(i, mirror_of[i]) for i in range(n) if keep(i // 2)]
        return lax.ppermute(x, "fsdp", pairs)

    def inner(chip):
        return chips // 4 <= chip < chips - chips // 4

    tiles = gate_pre.shape[1] // TILE
    blocks = {0: down_weight}
    step = 2
    while step < h:
        blocks.update({k ^ step: swap(v, "fsdp", n, step) for k, v in list(blocks.items())})
        step *= 2
    gate_inner = mirror(gate_pre, inner)
    cot_full = lax.all_gather(cotangent, "solve", axis=1, tiled=True)
    part = rows // m
    near = cot_full.shape[1] // 2
    quarter = lax.dynamic_slice(cot_full, (s * part, (1 - side) * near), (part, near))
    quarter = mirror(quarter)
    cot_far = lax.all_gather(quarter, "solve", axis=0, tiled=True)
    sibling = swap(down_weight, "fsdp", n, 1)
    blocks.update({k ^ 1: swap(v, "fsdp", n, 1) for k, v in list(blocks.items()) if k})
    blocks[1] = sibling
    order = sorted(blocks)
    weights = [blocks[k] for k in order]
    share = max(1, tiles // 7)
    cuts = [0, tiles - 3 * share, tiles - share, tiles]
    chunks = []
    for j, (a, b) in enumerate(zip(cuts[:-1], cuts[1:])):
        gate_outer, _ = lax.optimization_barrier((gate_pre[:, a * TILE : b * TILE], quarter))
        gate_outer = mirror(gate_outer, lambda chip: not inner(chip))
        chunks.append((j, a, b, gate_outer))

    gate = gate_pre.astype(f32)
    hidden = (gate * jax.nn.sigmoid(gate) * up_pre.astype(f32)).astype(jnp.bfloat16)
    early = jnp.concatenate(
        [
            jnp.dot(hidden, proj_hidden[:, :half], preferred_element_type=f32),
            jnp.dot(cotangent, proj_model[:, :half], preferred_element_type=f32),
            jnp.dot(inputs, proj_model[:, half:], preferred_element_type=f32),
        ],
        axis=1,
    )
    early = total(early, "solve", m)

    query_block = lax.all_gather(queries.astype(jnp.bfloat16), "fsdp", axis=1, tiled=True)
    partial = jnp.dot(inverse_factor, query_block.astype(f32), precision=lax.Precision.HIGH)
    whitened = partial
    bit = m // 2
    while bit:
        size = whitened.shape[0] // 2
        mine = s // bit % 2
        moved = swap(lax.dynamic_slice_in_dim(whitened, (1 - mine) * size, size, 0), "solve", m, bit)
        whitened = lax.dynamic_slice_in_dim(whitened, mine * size, size, 0) + moved
        bit //= 2
    whitened_rows = whitened
    bit = 1
    while bit < m:
        mine = s // bit % 2
        moved = swap(whitened_rows, "solve", m, bit)
        whitened_rows = jnp.where(
            mine == 0,
            jnp.concatenate([whitened_rows, moved], axis=0),
            jnp.concatenate([moved, whitened_rows], axis=0),
        )
        bit *= 2
    query_side = lax.dot_general(whitened_rows, inverse_factor, (((0,), (0,)), ((), ())), precision=lax.Precision.HIGH)

    own_idx = jnp.stack([f ^ k for k in order]).astype(jnp.int32)
    far_idx = own_idx - side * h
    other_side = swap(query_side, "fsdp", n, 1)
    own_idx, query_side, _ = lax.optimization_barrier((own_idx, query_side, quarter))
    own = tokens(
        own_idx, cot_full, [(v, 0) for v in weights], [(gate_pre, 0)], None, proj_hidden, 0, tiles
    )
    token_index = lax.broadcasted_iota(jnp.int32, (rows, 1), 0)
    slots = lax.broadcasted_iota(jnp.int32, (1, local_seqs), 1)
    length_of = jnp.sum(
        jnp.where(token_index // SEQ_LEN == slots, lengths[None, :], 0), axis=1, keepdims=True
    )
    weight_of = jnp.where(
        token_index % SEQ_LEN < length_of, 1.0 / jnp.sqrt(length_of.astype(f32)), 0.0
    )
    in_down = early[:, :half]
    out_down = early[:, half : 2 * half] * weight_of
    in_up = early[:, 2 * half :] * weight_of
    in_up_far = mirror(in_up.astype(jnp.bfloat16)).astype(f32)

    def pair(outs, ins):
        shape = (local_seqs, SEQ_LEN, half)
        feat = jnp.einsum("eto,eti->eoi", outs.reshape(shape), ins.reshape(shape), precision=top)
        return feat.reshape(local_seqs, half * half)

    down = pair(out_down, in_down)
    up_own = pair(own[:, half:], in_up)

    grad = gradient(far_idx, cot_far, weights)
    far = None
    for j, a, b, gate_outer in chunks:
        if far is not None:
            gate_outer, far = lax.optimization_barrier((gate_outer, far))
        units = slice(a * TILE, b * TILE)
        gate = gate_inner[:, units].astype(f32) + gate_outer.astype(f32)
        grad_up = (grad[:, units] * (gate * jax.nn.sigmoid(gate))).astype(jnp.bfloat16)
        term = jnp.dot(grad_up, proj_hidden[units, half:], preferred_element_type=f32)
        far = term if far is None else far + term
    up_far = pair(far, in_up_far)
    query_side = split(query_side + other_side)
    up = up_own + mirror(up_far)
    up = total(up, "solve", m)
    both = lax.all_gather(jnp.concatenate([up, down], axis=0), "fsdp", axis=0, tiled=True)

    examples = n * local_seqs
    row_width = gram.shape[0]
    col_width = gram.shape[1]
    count = queries.shape[1] * n
    size = half * half

    def place(offset):
        up_part = offset >= size
        shape = (examples, 2 * examples)
        row = lax.broadcasted_iota(jnp.int32, shape, 0)
        column = lax.broadcasted_iota(jnp.int32, shape, 1)
        wanted = row // local_seqs * 2 * local_seqs + row % local_seqs + jnp.where(up_part, 0, local_seqs)
        return (column == wanted).astype(jnp.bfloat16), jnp.where(up_part, offset - size, offset)

    pick_left, at_left = place(f * row_width)
    pick_right, at_right = place(s * col_width)
    at = jnp.stack([at_left, at_right]).astype(jnp.int32)
    left, right, scores = pl.pallas_call(
        functools.partial(features_kernel, 1.0 / math.sqrt(2 * size)),
        out_shape=(
            jax.ShapeDtypeStruct((3 * examples, row_width), jnp.bfloat16),
            jax.ShapeDtypeStruct((3 * examples, col_width), jnp.bfloat16),
            jax.ShapeDtypeStruct((examples, count), f32),
        ),
        in_specs=[pl.BlockSpec(memory_space=pltpu.SMEM)] + [pl.BlockSpec(memory_space=pltpu.VMEM)] * 5,
    )(at, both, pick_left, pick_right, *query_side)
    scores = total(scores, "fsdp", n, 2)
    scores = total(scores, "solve", m)
    block = 128
    steps = row_width // block
    ends = [0, steps // 2, steps]
    new_gram = None
    for a, b in zip(ends[:-1], ends[1:]):
        in_specs = [
            pl.BlockSpec((block, col_width), functools.partial(lambda z, i: (z + i, 0), a)),
            pl.BlockSpec((3 * examples, block), functools.partial(lambda z, i: (0, z + i), a)),
            pl.BlockSpec((3 * examples, col_width), lambda i: (0, 0)),
        ]
        operands = [gram, left, right]
        if new_gram is not None:
            in_specs.append(pl.BlockSpec(memory_space=pl.ANY))
            operands.append(new_gram)
        new_gram = pl.pallas_call(
            functools.partial(gram_kernel, 1.0 / examples),
            out_shape=jax.ShapeDtypeStruct(gram.shape, f32),
            grid=(b - a,),
            in_specs=in_specs,
            out_specs=pl.BlockSpec((block, col_width), functools.partial(lambda z, i: (z + i, 0), a)),
            input_output_aliases={} if new_gram is None else {3: 0},
        )(*operands)
    return (new_gram, whitened, scores)


def solution(mesh):
    in_specs = (
        P("fsdp", "solve"),
        P("fsdp", "solve"),
        P("fsdp", "solve"),
        P("fsdp", "solve"),
        P("solve", "fsdp"),
        P("solve", None),
        P("solve", None),
        P("fsdp"),
        P("fsdp", "solve"),
        P("fsdp", "solve"),
        P("solve", "fsdp"),
    )
    out_specs = (P("fsdp", "solve"), P(("fsdp", "solve"), None), P())

    def body(*args):
        return local(mesh.shape["fsdp"], mesh.shape["solve"], *args)

    return jax.shard_map(body, mesh=mesh, in_specs=in_specs, out_specs=out_specs, check_vma=False)
```

```python
import functools
import math

import jax
import jax.numpy as jnp
from jax import lax
from jax.experimental import pallas as pl
from jax.experimental.pallas import tpu as pltpu
from jax.sharding import PartitionSpec as P


SEQ_LEN = 256
TILE = 256


def tokens_kernel(count, gates, chained, idx, *refs):
    del idx
    cots, refs = refs[:count], refs[count:]
    weights, refs = refs[:count], refs[count:]
    gate_refs, refs = refs[:gates], refs[gates:]
    if chained:
        start, refs = refs[0], refs[1:]
    proj, out = refs

    @pl.when(pl.program_id(0) == 0)
    def _():
        out[...] = start[...] if chained else jnp.zeros_like(out)

    grad = None
    for cot, weight in zip(cots, weights):
        term = lax.dot_general(
            cot[...], weight[...], (((1,), (1,)), ((), ())), preferred_element_type=jnp.float32
        )
        grad = term if grad is None else grad + term
    gate = gate_refs[0][...].astype(jnp.float32)
    for other in gate_refs[1:]:
        gate = gate + other[...].astype(jnp.float32)
    smooth = gate * jax.nn.sigmoid(gate)
    grad_up = (grad * smooth).astype(jnp.bfloat16)
    out[...] += jnp.dot(grad_up, proj[...], preferred_element_type=jnp.float32)


def tokens(idx, cot, weights, gate_parts, start, proj, first, tiles):
    count = len(weights)
    rows = cot.shape[0]
    width = weights[0][0].shape[1]
    in_specs = [
        pl.BlockSpec(
            (rows, width), functools.partial(lambda k, i, ix: (0, ix[k]), k), pipeline_mode=pl.Buffered(1)
        )
        for k in range(count)
    ]
    for _, shift in weights:
        in_specs.append(pl.BlockSpec((TILE, width), functools.partial(lambda a, i, ix: (a + i, 0), shift)))
    for _, shift in gate_parts:
        in_specs.append(pl.BlockSpec((rows, TILE), functools.partial(lambda a, i, ix: (0, a + i), shift)))
    operands = [cot] * count + [part for part, _ in weights] + [part for part, _ in gate_parts]
    whole = pl.BlockSpec((rows, proj.shape[1]), lambda i, ix: (0, 0))
    if start is not None:
        in_specs.append(whole)
        operands.append(start)
    in_specs.append(pl.BlockSpec((TILE, proj.shape[1]), lambda i, ix: (first + i, 0)))
    operands.append(proj)
    return pl.pallas_call(
        functools.partial(tokens_kernel, count, len(gate_parts), start is not None),
        out_shape=jax.ShapeDtypeStruct((rows, proj.shape[1]), jnp.float32),
        grid_spec=pltpu.PrefetchScalarGridSpec(
            num_scalar_prefetch=1,
            grid=(tiles,),
            in_specs=in_specs,
            out_specs=whole,
        ),
        compiler_params=pltpu.CompilerParams(dimension_semantics=("arbitrary",)),
        cost_estimate=pl.CostEstimate(
            flops=2 * rows * TILE * tiles * (count * width + 256),
            bytes_accessed=TILE * tiles * (count * width + 2 * rows) * 2 + rows * count * width * 2,
            transcendentals=rows * TILE * tiles,
        ),
    )(idx, *operands)


def grad_kernel(count, idx, *refs):
    del idx
    out = refs[-1]
    grad = None
    for cot, weight in zip(refs[:count], refs[count : 2 * count]):
        term = lax.dot_general(
            cot[...], weight[...], (((1,), (1,)), ((), ())), preferred_element_type=jnp.float32
        )
        grad = term if grad is None else grad + term
    out[...] = grad


def gradient(idx, cot, weights):
    count = len(weights)
    rows = cot.shape[0]
    units, width = weights[0].shape
    in_specs = [
        pl.BlockSpec(
            (rows, width), functools.partial(lambda k, i, ix: (0, ix[k]), k), pipeline_mode=pl.Buffered(1)
        )
        for k in range(count)
    ]
    in_specs += [pl.BlockSpec((TILE, width), lambda i, ix: (i, 0))] * count
    return pl.pallas_call(
        functools.partial(grad_kernel, count),
        out_shape=jax.ShapeDtypeStruct((rows, units), jnp.float32),
        grid_spec=pltpu.PrefetchScalarGridSpec(
            num_scalar_prefetch=1,
            grid=(units // TILE,),
            in_specs=in_specs,
            out_specs=pl.BlockSpec((rows, TILE), lambda i, ix: (0, i)),
        ),
        compiler_params=pltpu.CompilerParams(dimension_semantics=("arbitrary",)),
        cost_estimate=pl.CostEstimate(
            flops=2 * rows * units * count * width,
            bytes_accessed=units * count * width * 2 + rows * count * width * 2 + rows * units * 4,
            transcendentals=0,
        ),
    )(idx, *([cot] * count), *weights)


def split(x):
    high = x.astype(jnp.bfloat16)
    return high, (x - high.astype(jnp.float32)).astype(jnp.bfloat16)


def features_kernel(scale, idx, both, pick_left, pick_right, high_side, low_side, left_out, right_out, scores):
    f32 = jnp.float32

    def part(offset, width, pick):
        at = pl.multiple_of(offset, 128)
        high, low = split(jnp.concatenate([both[i, :, pl.ds(at, width)] for i in range(both.shape[0])], axis=0))
        return jnp.dot(pick, high, preferred_element_type=f32) + jnp.dot(pick, low, preferred_element_type=f32)

    def against(x, side):
        return lax.dot_general(x, side, (((1,), (1,)), ((), ())), preferred_element_type=f32)

    high, low = split(part(idx[0], left_out.shape[1], pick_left[...]))
    left_out[...] = jnp.concatenate([high, low, high], axis=0)
    high, low = split(part(idx[1], right_out.shape[1], pick_right[...]))
    right_out[...] = jnp.concatenate([high, high, low], axis=0)
    product = against(high, high_side[...]) + (against(low, high_side[...]) + against(high, low_side[...]))
    scores[...] = product * scale


def gram_kernel(scale, gram, left, right, *refs):
    out = refs[-1]
    term = lax.dot_general(
        left[...], right[...], (((0,), (0,)), ((), ())), preferred_element_type=jnp.float32
    )
    out[...] = gram[...] + term * scale


def local(
    n,
    m,
    inputs,
    cotangent,
    gate_pre,
    up_pre,
    down_weight,
    proj_model,
    proj_hidden,
    lengths,
    gram,
    inverse_factor,
    queries,
):
    top = lax.Precision.HIGHEST
    f32 = jnp.float32
    f = lax.axis_index("fsdp")
    s = lax.axis_index("solve")
    rows = inputs.shape[0]
    local_seqs = lengths.shape[0]
    half = proj_model.shape[1] // 2
    h = n // 2
    chips = n // 2
    side = f // h

    def swap(x, axis, size, bit):
        return lax.ppermute(x, axis, [(i, i ^ bit) for i in range(size)])

    def total(x, axis, size, bit=1):
        while bit < size:
            if 2 * bit < size:
                one, two, both = (swap(x, axis, size, b) for b in (bit, 2 * bit, 3 * bit))
                x = (x + one) + (two + both)
            else:
                x = x + swap(x, axis, size, bit)
            bit *= 4
        return x

    mirror_of = [(chips - 1 - i // 2) * 2 + i % 2 for i in range(n)]

    def mirror(x, keep=lambda chip: True):
        pairs = [(i, mirror_of[i]) for i in range(n) if keep(i // 2)]
        return lax.ppermute(x, "fsdp", pairs)

    def inner(chip):
        return chips // 4 <= chip < chips - chips // 4

    tiles = gate_pre.shape[1] // TILE
    blocks = {0: down_weight}
    step = 2
    while step < h:
        blocks.update({k ^ step: swap(v, "fsdp", n, step) for k, v in list(blocks.items())})
        step *= 2
    head = tiles * 9 // 14
    gate_inner_a = mirror(gate_pre[:, : head * TILE], inner)
    part = rows // m
    cot_full = lax.all_gather(cotangent, "solve", axis=1, tiled=True)
    near = cot_full.shape[1] // 2
    quarter = lax.all_to_all(cotangent, "solve", split_axis=0, concat_axis=1, tiled=True)
    quarter = lax.dynamic_slice(quarter, (0, (1 - side) * near), (part, near))
    quarter = mirror(quarter)
    gate_inner_b = mirror(gate_pre[:, head * TILE :], inner)
    cot_far = lax.all_gather(quarter, "solve", axis=0, tiled=True)
    sibling = swap(down_weight, "fsdp", n, 1)
    blocks.update({k ^ 1: swap(v, "fsdp", n, 1) for k, v in list(blocks.items()) if k})
    blocks[1] = sibling
    order = sorted(blocks)
    weights = [blocks[k] for k in order]
    share = max(1, tiles // 7)
    cuts = [0, head, tiles - share, tiles]
    chunks = []
    for j, (a, b) in enumerate(zip(cuts[:-1], cuts[1:])):
        gate_outer = mirror(gate_pre[:, a * TILE : b * TILE], lambda chip: not inner(chip))
        chunks.append((j, a, b, gate_outer))

    gate = gate_pre.astype(f32)
    hidden = (gate * jax.nn.sigmoid(gate) * up_pre.astype(f32)).astype(jnp.bfloat16)
    early = jnp.concatenate(
        [
            jnp.dot(hidden, proj_hidden[:, :half], preferred_element_type=f32),
            jnp.dot(cotangent, proj_model[:, :half], preferred_element_type=f32),
            jnp.dot(inputs, proj_model[:, half:], preferred_element_type=f32),
        ],
        axis=1,
    )
    early = total(early, "solve", m)

    query_block = lax.all_gather(queries.astype(jnp.bfloat16), "fsdp", axis=1, tiled=True)
    partial = jnp.dot(inverse_factor, query_block.astype(f32), precision=lax.Precision.HIGH)
    whitened = partial
    bit = m // 2
    while bit:
        size = whitened.shape[0] // 2
        mine = s // bit % 2
        moved = swap(lax.dynamic_slice_in_dim(whitened, (1 - mine) * size, size, 0), "solve", m, bit)
        whitened = lax.dynamic_slice_in_dim(whitened, mine * size, size, 0) + moved
        bit //= 2
    whitened_rows = whitened
    bit = 1
    while bit < m:
        mine = s // bit % 2
        moved = swap(whitened_rows, "solve", m, bit)
        whitened_rows = jnp.where(
            mine == 0,
            jnp.concatenate([whitened_rows, moved], axis=0),
            jnp.concatenate([moved, whitened_rows], axis=0),
        )
        bit *= 2
    query_side = lax.dot_general(whitened_rows, inverse_factor, (((0,), (0,)), ((), ())), precision=lax.Precision.HIGH)

    own_idx = jnp.stack([f ^ k for k in order]).astype(jnp.int32)
    far_idx = own_idx - side * h
    other_side = swap(query_side, "fsdp", n, 1)
    own_idx, _ = lax.optimization_barrier((own_idx, quarter))
    far_idx, query_side = lax.optimization_barrier((far_idx, query_side))
    own = tokens(
        own_idx, cot_full, [(v, 0) for v in weights], [(gate_pre, 0)], None, proj_hidden, 0, tiles
    )
    token_index = lax.broadcasted_iota(jnp.int32, (rows, 1), 0)
    slots = lax.broadcasted_iota(jnp.int32, (1, local_seqs), 1)
    length_of = jnp.sum(
        jnp.where(token_index // SEQ_LEN == slots, lengths[None, :], 0), axis=1, keepdims=True
    )
    weight_of = jnp.where(
        token_index % SEQ_LEN < length_of, 1.0 / jnp.sqrt(length_of.astype(f32)), 0.0
    )
    in_down = early[:, :half]
    out_down = early[:, half : 2 * half] * weight_of
    in_up = early[:, 2 * half :] * weight_of
    in_up_far = mirror(in_up.astype(jnp.bfloat16)).astype(f32)

    def pair(outs, ins):
        shape = (local_seqs, SEQ_LEN, half)
        feat = jnp.einsum("eto,eti->eoi", outs.reshape(shape), ins.reshape(shape), precision=top)
        return feat.reshape(local_seqs, half * half)

    down = pair(out_down, in_down)
    up_own = pair(own[:, half:], in_up)

    grad = gradient(far_idx, cot_far, weights)
    far = None
    for j, a, b, gate_outer in chunks:
        if far is not None:
            gate_outer, far = lax.optimization_barrier((gate_outer, far))
        units = slice(a * TILE, b * TILE)
        gate_inner = gate_inner_a if b <= head else gate_inner_b[:, (a - head) * TILE : (b - head) * TILE]
        gate = gate_inner.astype(f32) + gate_outer.astype(f32)
        grad_up = (grad[:, units] * (gate * jax.nn.sigmoid(gate))).astype(jnp.bfloat16)
        term = jnp.dot(grad_up, proj_hidden[units, half:], preferred_element_type=f32)
        far = term if far is None else far + term
    up_far = pair(far, in_up_far)
    query_side = query_side + other_side
    high = lax.reduce_precision(query_side, 8, 7)
    query_side = (high.astype(jnp.bfloat16), (query_side - high).astype(jnp.bfloat16))
    up = up_own + mirror(up_far)
    up = total(up, "solve", m)
    both = lax.all_gather(jnp.concatenate([up, down], axis=0), "fsdp", axis=0)

    examples = n * local_seqs
    row_width = gram.shape[0]
    col_width = gram.shape[1]
    count = queries.shape[1] * n
    size = half * half

    def place(offset):
        up_part = offset >= size
        shape = (examples, 2 * examples)
        row = lax.broadcasted_iota(jnp.int32, shape, 0)
        column = lax.broadcasted_iota(jnp.int32, shape, 1)
        wanted = row // local_seqs * 2 * local_seqs + row % local_seqs + jnp.where(up_part, 0, local_seqs)
        return (column == wanted).astype(jnp.bfloat16), jnp.where(up_part, offset - size, offset)

    pick_left, at_left = place(f * row_width)
    pick_right, at_right = place(s * col_width)
    at = jnp.stack([at_left, at_right]).astype(jnp.int32)
    left, right, scores = pl.pallas_call(
        functools.partial(features_kernel, 1.0 / math.sqrt(2 * size)),
        out_shape=(
            jax.ShapeDtypeStruct((3 * examples, row_width), jnp.bfloat16),
            jax.ShapeDtypeStruct((3 * examples, col_width), jnp.bfloat16),
            jax.ShapeDtypeStruct((examples, count), f32),
        ),
        in_specs=[pl.BlockSpec(memory_space=pltpu.SMEM)] + [pl.BlockSpec(memory_space=pltpu.VMEM)] * 5,
    )(at, both, pick_left, pick_right, *query_side)
    scores = total(scores, "fsdp", n, 2)
    scores = total(scores, "solve", m)
    block = 128
    steps = row_width // block
    ends = [0, steps // 2, steps]
    new_gram = None
    for a, b in zip(ends[:-1], ends[1:]):
        in_specs = [
            pl.BlockSpec((block, col_width), functools.partial(lambda z, i: (z + i, 0), a)),
            pl.BlockSpec((3 * examples, block), functools.partial(lambda z, i: (0, z + i), a)),
            pl.BlockSpec((3 * examples, col_width), lambda i: (0, 0)),
        ]
        operands = [gram, left, right]
        if new_gram is not None:
            in_specs.append(pl.BlockSpec(memory_space=pl.ANY))
            operands.append(new_gram)
        new_gram = pl.pallas_call(
            functools.partial(gram_kernel, 1.0 / examples),
            out_shape=jax.ShapeDtypeStruct(gram.shape, f32),
            grid=(b - a,),
            in_specs=in_specs,
            out_specs=pl.BlockSpec((block, col_width), functools.partial(lambda z, i: (z + i, 0), a)),
            input_output_aliases={} if new_gram is None else {3: 0},
        )(*operands)
    return (new_gram, whitened, scores)


def solution(mesh):
    in_specs = (
        P("fsdp", "solve"),
        P("fsdp", "solve"),
        P("fsdp", "solve"),
        P("fsdp", "solve"),
        P("solve", "fsdp"),
        P("solve", None),
        P("solve", None),
        P("fsdp"),
        P("fsdp", "solve"),
        P("fsdp", "solve"),
        P("solve", "fsdp"),
    )
    out_specs = (P("fsdp", "solve"), P(("fsdp", "solve"), None), P())

    def body(*args):
        return local(mesh.shape["fsdp"], mesh.shape["solve"], *args)

    return jax.shard_map(body, mesh=mesh, in_specs=in_specs, out_specs=out_specs, check_vma=False)
```

```python
import functools
import math

import jax
import jax.numpy as jnp
from jax import lax
from jax.experimental import pallas as pl
from jax.experimental.pallas import tpu as pltpu
from jax.sharding import PartitionSpec as P


SEQ_LEN = 256
TILE = 256


def tokens_kernel(count, gates, chained, idx, *refs):
    del idx
    cots, refs = refs[:count], refs[count:]
    weights, refs = refs[:count], refs[count:]
    gate_refs, refs = refs[:gates], refs[gates:]
    if chained:
        start, refs = refs[0], refs[1:]
    proj, out = refs

    @pl.when(pl.program_id(0) == 0)
    def _():
        out[...] = start[...] if chained else jnp.zeros_like(out)

    grad = None
    for cot, weight in zip(cots, weights):
        term = lax.dot_general(
            cot[...], weight[...], (((1,), (1,)), ((), ())), preferred_element_type=jnp.float32
        )
        grad = term if grad is None else grad + term
    gate = gate_refs[0][...].astype(jnp.float32)
    for other in gate_refs[1:]:
        gate = gate + other[...].astype(jnp.float32)
    smooth = gate * jax.nn.sigmoid(gate)
    grad_up = (grad * smooth).astype(jnp.bfloat16)
    out[...] += jnp.dot(grad_up, proj[...], preferred_element_type=jnp.float32)


def tokens(idx, cot, weights, gate_parts, start, proj, first, tiles):
    count = len(weights)
    rows = cot.shape[0]
    width = weights[0][0].shape[1]
    in_specs = [
        pl.BlockSpec(
            (rows, width), functools.partial(lambda k, i, ix: (0, ix[k]), k), pipeline_mode=pl.Buffered(1)
        )
        for k in range(count)
    ]
    for _, shift in weights:
        in_specs.append(pl.BlockSpec((TILE, width), functools.partial(lambda a, i, ix: (a + i, 0), shift)))
    for _, shift in gate_parts:
        in_specs.append(pl.BlockSpec((rows, TILE), functools.partial(lambda a, i, ix: (0, a + i), shift)))
    operands = [cot] * count + [part for part, _ in weights] + [part for part, _ in gate_parts]
    whole = pl.BlockSpec((rows, proj.shape[1]), lambda i, ix: (0, 0))
    if start is not None:
        in_specs.append(whole)
        operands.append(start)
    in_specs.append(pl.BlockSpec((TILE, proj.shape[1]), lambda i, ix: (first + i, 0)))
    operands.append(proj)
    return pl.pallas_call(
        functools.partial(tokens_kernel, count, len(gate_parts), start is not None),
        out_shape=jax.ShapeDtypeStruct((rows, proj.shape[1]), jnp.float32),
        grid_spec=pltpu.PrefetchScalarGridSpec(
            num_scalar_prefetch=1,
            grid=(tiles,),
            in_specs=in_specs,
            out_specs=whole,
        ),
        compiler_params=pltpu.CompilerParams(dimension_semantics=("arbitrary",)),
        cost_estimate=pl.CostEstimate(
            flops=2 * rows * TILE * tiles * (count * width + 256),
            bytes_accessed=TILE * tiles * (count * width + 2 * rows) * 2 + rows * count * width * 2,
            transcendentals=rows * TILE * tiles,
        ),
    )(idx, *operands)


def grad_kernel(count, idx, *refs):
    del idx
    out = refs[-1]
    grad = None
    for cot, weight in zip(refs[:count], refs[count : 2 * count]):
        term = lax.dot_general(
            cot[...], weight[...], (((1,), (1,)), ((), ())), preferred_element_type=jnp.float32
        )
        grad = term if grad is None else grad + term
    out[...] = grad


def gradient(idx, cot, weights):
    count = len(weights)
    rows = cot.shape[0]
    units, width = weights[0].shape
    in_specs = [
        pl.BlockSpec(
            (rows, width), functools.partial(lambda k, i, ix: (0, ix[k]), k), pipeline_mode=pl.Buffered(1)
        )
        for k in range(count)
    ]
    in_specs += [pl.BlockSpec((TILE, width), lambda i, ix: (i, 0))] * count
    return pl.pallas_call(
        functools.partial(grad_kernel, count),
        out_shape=jax.ShapeDtypeStruct((rows, units), jnp.float32),
        grid_spec=pltpu.PrefetchScalarGridSpec(
            num_scalar_prefetch=1,
            grid=(units // TILE,),
            in_specs=in_specs,
            out_specs=pl.BlockSpec((rows, TILE), lambda i, ix: (0, i)),
        ),
        compiler_params=pltpu.CompilerParams(dimension_semantics=("arbitrary",)),
        cost_estimate=pl.CostEstimate(
            flops=2 * rows * units * count * width,
            bytes_accessed=units * count * width * 2 + rows * count * width * 2 + rows * units * 4,
            transcendentals=0,
        ),
    )(idx, *([cot] * count), *weights)


def split(x):
    high = x.astype(jnp.bfloat16)
    return high, (x - high.astype(jnp.float32)).astype(jnp.bfloat16)


def features_kernel(scale, idx, both, pick_left, pick_right, high_side, low_side, left_out, right_out, scores):
    f32 = jnp.float32

    def part(offset, width, pick):
        at = pl.multiple_of(offset, 128)
        high, low = split(jnp.concatenate([both[i, :, pl.ds(at, width)] for i in range(both.shape[0])], axis=0))
        return jnp.dot(pick, high, preferred_element_type=f32) + jnp.dot(pick, low, preferred_element_type=f32)

    def against(x, side):
        return lax.dot_general(x, side, (((1,), (1,)), ((), ())), preferred_element_type=f32)

    high, low = split(part(idx[0], left_out.shape[1], pick_left[...]))
    left_out[...] = jnp.concatenate([high, low, high], axis=0)
    high, low = split(part(idx[1], right_out.shape[1], pick_right[...]))
    right_out[...] = jnp.concatenate([high, high, low], axis=0)
    product = against(high, high_side[...]) + (against(low, high_side[...]) + against(high, low_side[...]))
    scores[...] = product * scale


def gram_kernel(scale, gram, left, right, *refs):
    out = refs[-1]
    term = lax.dot_general(
        left[...], right[...], (((0,), (0,)), ((), ())), preferred_element_type=jnp.float32
    )
    out[...] = gram[...] + term * scale


def local(
    n,
    m,
    inputs,
    cotangent,
    gate_pre,
    up_pre,
    down_weight,
    proj_model,
    proj_hidden,
    lengths,
    gram,
    inverse_factor,
    queries,
):
    top = lax.Precision.HIGHEST
    f32 = jnp.float32
    f = lax.axis_index("fsdp")
    s = lax.axis_index("solve")
    rows = inputs.shape[0]
    local_seqs = lengths.shape[0]
    half = proj_model.shape[1] // 2
    h = n // 2
    chips = n // 2
    side = f // h

    def swap(x, axis, size, bit):
        return lax.ppermute(x, axis, [(i, i ^ bit) for i in range(size)])

    def total(x, axis, size, bit=1):
        while bit < size:
            if 2 * bit < size:
                one, two, both = (swap(x, axis, size, b) for b in (bit, 2 * bit, 3 * bit))
                x = (x + one) + (two + both)
            else:
                x = x + swap(x, axis, size, bit)
            bit *= 4
        return x

    mirror_of = [(chips - 1 - i // 2) * 2 + i % 2 for i in range(n)]

    def mirror(x, keep=lambda chip: True):
        pairs = [(i, mirror_of[i]) for i in range(n) if keep(i // 2)]
        return lax.ppermute(x, "fsdp", pairs)

    def inner(chip):
        return chips // 4 <= chip < chips - chips // 4

    tiles = gate_pre.shape[1] // TILE
    blocks = {0: down_weight}
    step = 2
    while step < h:
        blocks.update({k ^ step: swap(v, "fsdp", n, step) for k, v in list(blocks.items())})
        step *= 2
    gate_inner = mirror(gate_pre, inner)
    cot_full = lax.all_gather(cotangent, "solve", axis=1, tiled=True)
    part = rows // m
    near = cot_full.shape[1] // 2
    quarter = lax.dynamic_slice(cot_full, (s * part, (1 - side) * near), (part, near))
    quarter = mirror(quarter)
    cot_far = lax.all_gather(quarter, "solve", axis=0, tiled=True)
    sibling = swap(down_weight, "fsdp", n, 1)
    blocks.update({k ^ 1: swap(v, "fsdp", n, 1) for k, v in list(blocks.items()) if k})
    blocks[1] = sibling
    order = sorted(blocks)
    weights = [blocks[k] for k in order]
    share = max(1, tiles // 7)
    cuts = [0, tiles - 3 * share, tiles - share, tiles]
    chunks = []
    for j, (a, b) in enumerate(zip(cuts[:-1], cuts[1:])):
        gate_outer, _ = lax.optimization_barrier((gate_pre[:, a * TILE : b * TILE], quarter))
        gate_outer = mirror(gate_outer, lambda chip: not inner(chip))
        chunks.append((j, a, b, gate_outer))

    gate = gate_pre.astype(f32)
    hidden = (gate * jax.nn.sigmoid(gate) * up_pre.astype(f32)).astype(jnp.bfloat16)
    early = jnp.concatenate(
        [
            jnp.dot(hidden, proj_hidden[:, :half], preferred_element_type=f32),
            jnp.dot(cotangent, proj_model[:, :half], preferred_element_type=f32),
            jnp.dot(inputs, proj_model[:, half:], preferred_element_type=f32),
        ],
        axis=1,
    )
    early = total(early, "solve", m)

    query_block = lax.all_gather(queries.astype(jnp.bfloat16), "fsdp", axis=1, tiled=True)
    partial = jnp.dot(inverse_factor, query_block.astype(f32), precision=lax.Precision.HIGH)
    whitened = partial
    bit = m // 2
    while bit:
        size = whitened.shape[0] // 2
        mine = s // bit % 2
        moved = swap(lax.dynamic_slice_in_dim(whitened, (1 - mine) * size, size, 0), "solve", m, bit)
        whitened = lax.dynamic_slice_in_dim(whitened, mine * size, size, 0) + moved
        bit //= 2
    whitened_rows = whitened
    bit = 1
    while bit < m:
        mine = s // bit % 2
        moved = swap(whitened_rows, "solve", m, bit)
        whitened_rows = jnp.where(
            mine == 0,
            jnp.concatenate([whitened_rows, moved], axis=0),
            jnp.concatenate([moved, whitened_rows], axis=0),
        )
        bit *= 2
    query_side = lax.dot_general(whitened_rows, inverse_factor, (((0,), (0,)), ((), ())), precision=lax.Precision.HIGH)

    own_idx = jnp.stack([f ^ k for k in order]).astype(jnp.int32)
    far_idx = own_idx - side * h
    other_side = swap(query_side, "fsdp", n, 1)
    own_idx, query_side, _ = lax.optimization_barrier((own_idx, query_side, quarter))
    own = tokens(
        own_idx, cot_full, [(v, 0) for v in weights], [(gate_pre, 0)], None, proj_hidden, 0, tiles
    )
    token_index = lax.broadcasted_iota(jnp.int32, (rows, 1), 0)
    slots = lax.broadcasted_iota(jnp.int32, (1, local_seqs), 1)
    length_of = jnp.sum(
        jnp.where(token_index // SEQ_LEN == slots, lengths[None, :], 0), axis=1, keepdims=True
    )
    weight_of = jnp.where(
        token_index % SEQ_LEN < length_of, 1.0 / jnp.sqrt(length_of.astype(f32)), 0.0
    )
    in_down = early[:, :half]
    out_down = early[:, half : 2 * half] * weight_of
    in_up = early[:, 2 * half :] * weight_of
    in_up_far = mirror(in_up.astype(jnp.bfloat16)).astype(f32)

    def pair(outs, ins):
        shape = (local_seqs, SEQ_LEN, half)
        feat = jnp.einsum("eto,eti->eoi", outs.reshape(shape), ins.reshape(shape), precision=top)
        return feat.reshape(local_seqs, half * half)

    down = pair(out_down, in_down)
    up_own = pair(own[:, half:], in_up)

    grad = gradient(far_idx, cot_far, weights)
    far = None
    for j, a, b, gate_outer in chunks:
        if far is not None:
            gate_outer, far = lax.optimization_barrier((gate_outer, far))
        units = slice(a * TILE, b * TILE)
        gate = gate_inner[:, units].astype(f32) + gate_outer.astype(f32)
        grad_up = (grad[:, units] * (gate * jax.nn.sigmoid(gate))).astype(jnp.bfloat16)
        term = jnp.dot(grad_up, proj_hidden[units, half:], preferred_element_type=f32)
        far = term if far is None else far + term
    up_far = pair(far, in_up_far)
    query_side = query_side + other_side
    high = lax.reduce_precision(query_side, 8, 7)
    query_side = (high.astype(jnp.bfloat16), (query_side - high).astype(jnp.bfloat16))
    up = up_own + mirror(up_far)
    up = total(up, "solve", m)
    both = lax.all_gather(jnp.concatenate([up, down], axis=0), "fsdp", axis=0)

    examples = n * local_seqs
    row_width = gram.shape[0]
    col_width = gram.shape[1]
    count = queries.shape[1] * n
    size = half * half

    def place(offset):
        up_part = offset >= size
        shape = (examples, 2 * examples)
        row = lax.broadcasted_iota(jnp.int32, shape, 0)
        column = lax.broadcasted_iota(jnp.int32, shape, 1)
        wanted = row // local_seqs * 2 * local_seqs + row % local_seqs + jnp.where(up_part, 0, local_seqs)
        return (column == wanted).astype(jnp.bfloat16), jnp.where(up_part, offset - size, offset)

    pick_left, at_left = place(f * row_width)
    pick_right, at_right = place(s * col_width)
    at = jnp.stack([at_left, at_right]).astype(jnp.int32)
    left, right, scores = pl.pallas_call(
        functools.partial(features_kernel, 1.0 / math.sqrt(2 * size)),
        out_shape=(
            jax.ShapeDtypeStruct((3 * examples, row_width), jnp.bfloat16),
            jax.ShapeDtypeStruct((3 * examples, col_width), jnp.bfloat16),
            jax.ShapeDtypeStruct((examples, count), f32),
        ),
        in_specs=[pl.BlockSpec(memory_space=pltpu.SMEM)] + [pl.BlockSpec(memory_space=pltpu.VMEM)] * 5,
    )(at, both, pick_left, pick_right, *query_side)
    scores = total(scores, "fsdp", n, 2)
    scores = total(scores, "solve", m)
    block = 128
    steps = row_width // block
    ends = [0, steps // 2, steps]
    new_gram = None
    for a, b in zip(ends[:-1], ends[1:]):
        in_specs = [
            pl.BlockSpec((block, col_width), functools.partial(lambda z, i: (z + i, 0), a)),
            pl.BlockSpec((3 * examples, block), functools.partial(lambda z, i: (0, z + i), a)),
            pl.BlockSpec((3 * examples, col_width), lambda i: (0, 0)),
        ]
        operands = [gram, left, right]
        if new_gram is not None:
            in_specs.append(pl.BlockSpec(memory_space=pl.ANY))
            operands.append(new_gram)
        new_gram = pl.pallas_call(
            functools.partial(gram_kernel, 1.0 / examples),
            out_shape=jax.ShapeDtypeStruct(gram.shape, f32),
            grid=(b - a,),
            in_specs=in_specs,
            out_specs=pl.BlockSpec((block, col_width), functools.partial(lambda z, i: (z + i, 0), a)),
            input_output_aliases={} if new_gram is None else {3: 0},
        )(*operands)
    return (new_gram, whitened, scores)


def solution(mesh):
    in_specs = (
        P("fsdp", "solve"),
        P("fsdp", "solve"),
        P("fsdp", "solve"),
        P("fsdp", "solve"),
        P("solve", "fsdp"),
        P("solve", None),
        P("solve", None),
        P("fsdp"),
        P("fsdp", "solve"),
        P("fsdp", "solve"),
        P("solve", "fsdp"),
    )
    out_specs = (P("fsdp", "solve"), P(("fsdp", "solve"), None), P())

    def body(*args):
        return local(mesh.shape["fsdp"], mesh.shape["solve"], *args)

    return jax.shard_map(body, mesh=mesh, in_specs=in_specs, out_specs=out_specs, check_vma=False)
```

```python
import functools
import math

import jax
import jax.numpy as jnp
from jax import lax
from jax.experimental import pallas as pl
from jax.experimental.pallas import tpu as pltpu
from jax.sharding import PartitionSpec as P


SEQ_LEN = 256
TILE = 256


def tokens_kernel(count, gates, chained, idx, *refs):
    del idx
    cots, refs = refs[:count], refs[count:]
    weights, refs = refs[:count], refs[count:]
    gate_refs, refs = refs[:gates], refs[gates:]
    if chained:
        start, refs = refs[0], refs[1:]
    proj, out = refs

    @pl.when(pl.program_id(0) == 0)
    def _():
        out[...] = start[...] if chained else jnp.zeros_like(out)

    grad = None
    for cot, weight in zip(cots, weights):
        term = lax.dot_general(
            cot[...], weight[...], (((1,), (1,)), ((), ())), preferred_element_type=jnp.float32
        )
        grad = term if grad is None else grad + term
    gate = gate_refs[0][...].astype(jnp.float32)
    for other in gate_refs[1:]:
        gate = gate + other[...].astype(jnp.float32)
    smooth = gate * jax.nn.sigmoid(gate)
    grad_up = (grad * smooth).astype(jnp.bfloat16)
    out[...] += jnp.dot(grad_up, proj[...], preferred_element_type=jnp.float32)


def tokens(idx, cot, weights, gate_parts, start, proj, first, tiles):
    count = len(weights)
    rows = cot.shape[0]
    width = weights[0][0].shape[1]
    in_specs = [
        pl.BlockSpec(
            (rows, width), functools.partial(lambda k, i, ix: (0, ix[k]), k), pipeline_mode=pl.Buffered(1)
        )
        for k in range(count)
    ]
    for _, shift in weights:
        in_specs.append(pl.BlockSpec((TILE, width), functools.partial(lambda a, i, ix: (a + i, 0), shift)))
    for _, shift in gate_parts:
        in_specs.append(pl.BlockSpec((rows, TILE), functools.partial(lambda a, i, ix: (0, a + i), shift)))
    operands = [cot] * count + [part for part, _ in weights] + [part for part, _ in gate_parts]
    whole = pl.BlockSpec((rows, proj.shape[1]), lambda i, ix: (0, 0))
    if start is not None:
        in_specs.append(whole)
        operands.append(start)
    in_specs.append(pl.BlockSpec((TILE, proj.shape[1]), lambda i, ix: (first + i, 0)))
    operands.append(proj)
    return pl.pallas_call(
        functools.partial(tokens_kernel, count, len(gate_parts), start is not None),
        out_shape=jax.ShapeDtypeStruct((rows, proj.shape[1]), jnp.float32),
        grid_spec=pltpu.PrefetchScalarGridSpec(
            num_scalar_prefetch=1,
            grid=(tiles,),
            in_specs=in_specs,
            out_specs=whole,
        ),
        compiler_params=pltpu.CompilerParams(dimension_semantics=("arbitrary",)),
        cost_estimate=pl.CostEstimate(
            flops=2 * rows * TILE * tiles * (count * width + 256),
            bytes_accessed=TILE * tiles * (count * width + 2 * rows) * 2 + rows * count * width * 2,
            transcendentals=rows * TILE * tiles,
        ),
    )(idx, *operands)


def grad_kernel(count, idx, *refs):
    del idx
    out = refs[-1]
    grad = None
    for cot, weight in zip(refs[:count], refs[count : 2 * count]):
        term = lax.dot_general(
            cot[...], weight[...], (((1,), (1,)), ((), ())), preferred_element_type=jnp.float32
        )
        grad = term if grad is None else grad + term
    out[...] = grad


def gradient(idx, cot, weights):
    count = len(weights)
    rows = cot.shape[0]
    units, width = weights[0].shape
    in_specs = [
        pl.BlockSpec(
            (rows, width), functools.partial(lambda k, i, ix: (0, ix[k]), k), pipeline_mode=pl.Buffered(1)
        )
        for k in range(count)
    ]
    in_specs += [pl.BlockSpec((TILE, width), lambda i, ix: (i, 0))] * count
    return pl.pallas_call(
        functools.partial(grad_kernel, count),
        out_shape=jax.ShapeDtypeStruct((rows, units), jnp.float32),
        grid_spec=pltpu.PrefetchScalarGridSpec(
            num_scalar_prefetch=1,
            grid=(units // TILE,),
            in_specs=in_specs,
            out_specs=pl.BlockSpec((rows, TILE), lambda i, ix: (0, i)),
        ),
        compiler_params=pltpu.CompilerParams(dimension_semantics=("arbitrary",)),
        cost_estimate=pl.CostEstimate(
            flops=2 * rows * units * count * width,
            bytes_accessed=units * count * width * 2 + rows * count * width * 2 + rows * units * 4,
            transcendentals=0,
        ),
    )(idx, *([cot] * count), *weights)


def split(x):
    high = x.astype(jnp.bfloat16)
    return high, (x - high.astype(jnp.float32)).astype(jnp.bfloat16)


def features_kernel(scale, idx, both, pick_left, pick_right, high_side, low_side, left_out, right_out, scores):
    f32 = jnp.float32

    def part(offset, width, pick):
        at = pl.multiple_of(offset, 128)
        high, low = split(jnp.concatenate([both[i, :, pl.ds(at, width)] for i in range(both.shape[0])], axis=0))
        return jnp.dot(pick, high, preferred_element_type=f32) + jnp.dot(pick, low, preferred_element_type=f32)

    def against(x, side):
        return lax.dot_general(x, side, (((1,), (1,)), ((), ())), preferred_element_type=f32)

    high, low = split(part(idx[0], left_out.shape[1], pick_left[...]))
    left_out[...] = jnp.concatenate([high, low, high], axis=0)
    high, low = split(part(idx[1], right_out.shape[1], pick_right[...]))
    right_out[...] = jnp.concatenate([high, high, low], axis=0)
    product = against(high, high_side[...]) + (against(low, high_side[...]) + against(high, low_side[...]))
    scores[...] = product * scale


def gram_kernel(scale, gram, left, right, *refs):
    out = refs[-1]
    term = lax.dot_general(
        left[...], right[...], (((0,), (0,)), ((), ())), preferred_element_type=jnp.float32
    )
    out[...] = gram[...] + term * scale


def local(
    n,
    m,
    inputs,
    cotangent,
    gate_pre,
    up_pre,
    down_weight,
    proj_model,
    proj_hidden,
    lengths,
    gram,
    inverse_factor,
    queries,
):
    top = lax.Precision.HIGHEST
    f32 = jnp.float32
    f = lax.axis_index("fsdp")
    s = lax.axis_index("solve")
    rows = inputs.shape[0]
    local_seqs = lengths.shape[0]
    half = proj_model.shape[1] // 2
    h = n // 2
    chips = n // 2
    side = f // h

    def swap(x, axis, size, bit):
        return lax.ppermute(x, axis, [(i, i ^ bit) for i in range(size)])

    def total(x, axis, size, bit=1):
        while bit < size:
            if 2 * bit < size:
                one, two, both = (swap(x, axis, size, b) for b in (bit, 2 * bit, 3 * bit))
                x = (x + one) + (two + both)
            else:
                x = x + swap(x, axis, size, bit)
            bit *= 4
        return x

    mirror_of = [(chips - 1 - i // 2) * 2 + i % 2 for i in range(n)]

    def mirror(x, keep=lambda chip: True):
        pairs = [(i, mirror_of[i]) for i in range(n) if keep(i // 2)]
        return lax.ppermute(x, "fsdp", pairs)

    def inner(chip):
        return chips // 4 <= chip < chips - chips // 4

    tiles = gate_pre.shape[1] // TILE
    blocks = {0: down_weight}
    step = 2
    while step < h:
        blocks.update({k ^ step: swap(v, "fsdp", n, step) for k, v in list(blocks.items())})
        step *= 2
    gate_inner = mirror(gate_pre, inner)
    cot_full = lax.all_gather(cotangent, "solve", axis=1, tiled=True)
    part = rows // m
    near = cot_full.shape[1] // 2
    quarter = lax.dynamic_slice(cot_full, (s * part, (1 - side) * near), (part, near))
    quarter = mirror(quarter)
    cot_far = lax.all_gather(quarter, "solve", axis=0, tiled=True)
    sibling = swap(down_weight, "fsdp", n, 1)
    blocks.update({k ^ 1: swap(v, "fsdp", n, 1) for k, v in list(blocks.items()) if k})
    blocks[1] = sibling
    order = sorted(blocks)
    weights = [blocks[k] for k in order]
    share = max(1, tiles // 7)
    cuts = [0, tiles - 3 * share, tiles - share, tiles]
    chunks = []
    for j, (a, b) in enumerate(zip(cuts[:-1], cuts[1:])):
        gate_outer, _ = lax.optimization_barrier((gate_pre[:, a * TILE : b * TILE], quarter))
        gate_outer = mirror(gate_outer, lambda chip: not inner(chip))
        chunks.append((j, a, b, gate_outer))

    gate = gate_pre.astype(f32)
    hidden = (gate * jax.nn.sigmoid(gate) * up_pre.astype(f32)).astype(jnp.bfloat16)
    early = jnp.concatenate(
        [
            jnp.dot(hidden, proj_hidden[:, :half], preferred_element_type=f32),
            jnp.dot(cotangent, proj_model[:, :half], preferred_element_type=f32),
            jnp.dot(inputs, proj_model[:, half:], preferred_element_type=f32),
        ],
        axis=1,
    )
    early = total(early, "solve", m)

    query_block = lax.all_gather(queries.astype(jnp.bfloat16), "fsdp", axis=1, tiled=True)
    partial = jnp.dot(inverse_factor, query_block.astype(f32), precision=lax.Precision.HIGH)
    whitened = partial
    bit = m // 2
    while bit:
        size = whitened.shape[0] // 2
        mine = s // bit % 2
        moved = swap(lax.dynamic_slice_in_dim(whitened, (1 - mine) * size, size, 0), "solve", m, bit)
        whitened = lax.dynamic_slice_in_dim(whitened, mine * size, size, 0) + moved
        bit //= 2
    whitened_rows = whitened
    bit = 1
    while bit < m:
        mine = s // bit % 2
        moved = swap(whitened_rows, "solve", m, bit)
        whitened_rows = jnp.where(
            mine == 0,
            jnp.concatenate([whitened_rows, moved], axis=0),
            jnp.concatenate([moved, whitened_rows], axis=0),
        )
        bit *= 2
    whitened_rows = lax.optimization_barrier(whitened_rows)
    query_side = lax.dot_general(whitened_rows, inverse_factor, (((0,), (0,)), ((), ())), precision=lax.Precision.HIGH)

    own_idx = jnp.stack([f ^ k for k in order]).astype(jnp.int32)
    far_idx = own_idx - side * h
    other_side = swap(query_side, "fsdp", n, 1)
    own_idx, query_side, _ = lax.optimization_barrier((own_idx, query_side, quarter))
    own = tokens(
        own_idx, cot_full, [(v, 0) for v in weights], [(gate_pre, 0)], None, proj_hidden, 0, tiles
    )
    token_index = lax.broadcasted_iota(jnp.int32, (rows, 1), 0)
    slots = lax.broadcasted_iota(jnp.int32, (1, local_seqs), 1)
    length_of = jnp.sum(
        jnp.where(token_index // SEQ_LEN == slots, lengths[None, :], 0), axis=1, keepdims=True
    )
    weight_of = jnp.where(
        token_index % SEQ_LEN < length_of, 1.0 / jnp.sqrt(length_of.astype(f32)), 0.0
    )
    in_down = early[:, :half]
    out_down = early[:, half : 2 * half] * weight_of
    in_up = early[:, 2 * half :] * weight_of
    in_up_far = mirror(lax.dynamic_slice_in_dim(in_up.astype(jnp.bfloat16), s * part, part, 0))

    def pair(outs, ins):
        shape = (local_seqs, SEQ_LEN, half)
        feat = jnp.einsum("eto,eti->eoi", outs.reshape(shape), ins.reshape(shape), precision=top)
        return feat.reshape(local_seqs, half * half)

    down = pair(out_down, in_down)
    up_own = pair(own[:, half:], in_up)

    grad = gradient(far_idx, cot_far, weights)
    far = None
    for j, a, b, gate_outer in chunks:
        if far is not None:
            gate_outer, far = lax.optimization_barrier((gate_outer, far))
        units = slice(a * TILE, b * TILE)
        gate = gate_inner[:, units].astype(f32) + gate_outer.astype(f32)
        grad_up = (grad[:, units] * (gate * jax.nn.sigmoid(gate))).astype(jnp.bfloat16)
        term = jnp.dot(grad_up, proj_hidden[units, half:], preferred_element_type=f32)
        far = term if far is None else far + term
        if j == len(chunks) - 2:
            far, in_up_far = lax.optimization_barrier((far, in_up_far))
            in_up_far = lax.all_gather(in_up_far, "solve", axis=0, tiled=True)
    up_far = pair(far, in_up_far.astype(f32))
    query_side = query_side + other_side
    high = lax.reduce_precision(query_side, 8, 7)
    query_side = (high.astype(jnp.bfloat16), (query_side - high).astype(jnp.bfloat16))
    up = up_own + mirror(up_far)
    up = total(up, "solve", m)
    both = lax.all_gather(jnp.concatenate([up, down], axis=0), "fsdp", axis=0)

    examples = n * local_seqs
    row_width = gram.shape[0]
    col_width = gram.shape[1]
    count = queries.shape[1] * n
    size = half * half

    def place(offset):
        up_part = offset >= size
        shape = (examples, 2 * examples)
        row = lax.broadcasted_iota(jnp.int32, shape, 0)
        column = lax.broadcasted_iota(jnp.int32, shape, 1)
        wanted = row // local_seqs * 2 * local_seqs + row % local_seqs + jnp.where(up_part, 0, local_seqs)
        return (column == wanted).astype(jnp.bfloat16), jnp.where(up_part, offset - size, offset)

    pick_left, at_left = place(f * row_width)
    pick_right, at_right = place(s * col_width)
    at = jnp.stack([at_left, at_right]).astype(jnp.int32)
    left, right, scores = pl.pallas_call(
        functools.partial(features_kernel, 1.0 / math.sqrt(2 * size)),
        out_shape=(
            jax.ShapeDtypeStruct((3 * examples, row_width), jnp.bfloat16),
            jax.ShapeDtypeStruct((3 * examples, col_width), jnp.bfloat16),
            jax.ShapeDtypeStruct((examples, count), f32),
        ),
        in_specs=[pl.BlockSpec(memory_space=pltpu.SMEM)] + [pl.BlockSpec(memory_space=pltpu.VMEM)] * 5,
    )(at, both, pick_left, pick_right, *query_side)
    scores = total(scores, "fsdp", n, 2)
    scores = total(scores, "solve", m)
    block = 128
    steps = row_width // block
    ends = [0, steps // 2, steps]
    new_gram = None
    for a, b in zip(ends[:-1], ends[1:]):
        in_specs = [
            pl.BlockSpec((block, col_width), functools.partial(lambda z, i: (z + i, 0), a)),
            pl.BlockSpec((3 * examples, block), functools.partial(lambda z, i: (0, z + i), a)),
            pl.BlockSpec((3 * examples, col_width), lambda i: (0, 0)),
        ]
        operands = [gram, left, right]
        if new_gram is not None:
            in_specs.append(pl.BlockSpec(memory_space=pl.ANY))
            operands.append(new_gram)
        new_gram = pl.pallas_call(
            functools.partial(gram_kernel, 1.0 / examples),
            out_shape=jax.ShapeDtypeStruct(gram.shape, f32),
            grid=(b - a,),
            in_specs=in_specs,
            out_specs=pl.BlockSpec((block, col_width), functools.partial(lambda z, i: (z + i, 0), a)),
            input_output_aliases={} if new_gram is None else {3: 0},
        )(*operands)
    return (new_gram, whitened, scores)


def solution(mesh):
    in_specs = (
        P("fsdp", "solve"),
        P("fsdp", "solve"),
        P("fsdp", "solve"),
        P("fsdp", "solve"),
        P("solve", "fsdp"),
        P("solve", None),
        P("solve", None),
        P("fsdp"),
        P("fsdp", "solve"),
        P("fsdp", "solve"),
        P("solve", "fsdp"),
    )
    out_specs = (P("fsdp", "solve"), P(("fsdp", "solve"), None), P())

    def body(*args):
        return local(mesh.shape["fsdp"], mesh.shape["solve"], *args)

    return jax.shard_map(body, mesh=mesh, in_specs=in_specs, out_specs=out_specs, check_vma=False)
```

```python
import functools
import math

import jax
import jax.numpy as jnp
from jax import lax
from jax.experimental import pallas as pl
from jax.experimental.pallas import tpu as pltpu
from jax.sharding import PartitionSpec as P


SEQ_LEN = 256
TILE = 256


def tokens_kernel(count, gates, chained, idx, *refs):
    del idx
    cots, refs = refs[:count], refs[count:]
    weights, refs = refs[:count], refs[count:]
    gate_refs, refs = refs[:gates], refs[gates:]
    if chained:
        start, refs = refs[0], refs[1:]
    proj, out = refs

    @pl.when(pl.program_id(0) == 0)
    def _():
        out[...] = start[...] if chained else jnp.zeros_like(out)

    grad = None
    for cot, weight in zip(cots, weights):
        term = lax.dot_general(
            cot[...], weight[...], (((1,), (1,)), ((), ())), preferred_element_type=jnp.float32
        )
        grad = term if grad is None else grad + term
    gate = gate_refs[0][...].astype(jnp.float32)
    for other in gate_refs[1:]:
        gate = gate + other[...].astype(jnp.float32)
    smooth = gate * jax.nn.sigmoid(gate)
    grad_up = (grad * smooth).astype(jnp.bfloat16)
    out[...] += jnp.dot(grad_up, proj[...], preferred_element_type=jnp.float32)


def tokens(idx, cot, weights, gate_parts, start, proj, first, tiles):
    count = len(weights)
    rows = cot.shape[0]
    width = weights[0][0].shape[1]
    in_specs = [
        pl.BlockSpec(
            (rows, width), functools.partial(lambda k, i, ix: (0, ix[k]), k), pipeline_mode=pl.Buffered(1)
        )
        for k in range(count)
    ]
    for _, shift in weights:
        in_specs.append(pl.BlockSpec((TILE, width), functools.partial(lambda a, i, ix: (a + i, 0), shift)))
    for _, shift in gate_parts:
        in_specs.append(pl.BlockSpec((rows, TILE), functools.partial(lambda a, i, ix: (0, a + i), shift)))
    operands = [cot] * count + [part for part, _ in weights] + [part for part, _ in gate_parts]
    whole = pl.BlockSpec((rows, proj.shape[1]), lambda i, ix: (0, 0))
    if start is not None:
        in_specs.append(whole)
        operands.append(start)
    in_specs.append(pl.BlockSpec((TILE, proj.shape[1]), lambda i, ix: (first + i, 0)))
    operands.append(proj)
    return pl.pallas_call(
        functools.partial(tokens_kernel, count, len(gate_parts), start is not None),
        out_shape=jax.ShapeDtypeStruct((rows, proj.shape[1]), jnp.float32),
        grid_spec=pltpu.PrefetchScalarGridSpec(
            num_scalar_prefetch=1,
            grid=(tiles,),
            in_specs=in_specs,
            out_specs=whole,
        ),
        compiler_params=pltpu.CompilerParams(dimension_semantics=("arbitrary",)),
        cost_estimate=pl.CostEstimate(
            flops=2 * rows * TILE * tiles * (count * width + 256),
            bytes_accessed=TILE * tiles * (count * width + 2 * rows) * 2 + rows * count * width * 2,
            transcendentals=rows * TILE * tiles,
        ),
    )(idx, *operands)


def grad_kernel(count, idx, *refs):
    del idx
    out = refs[-1]
    grad = None
    for cot, weight in zip(refs[:count], refs[count : 2 * count]):
        term = lax.dot_general(
            cot[...], weight[...], (((1,), (1,)), ((), ())), preferred_element_type=jnp.float32
        )
        grad = term if grad is None else grad + term
    out[...] = grad


def gradient(idx, cot, weights):
    count = len(weights)
    rows = cot.shape[0]
    units, width = weights[0].shape
    in_specs = [
        pl.BlockSpec(
            (rows, width), functools.partial(lambda k, i, ix: (0, ix[k]), k), pipeline_mode=pl.Buffered(1)
        )
        for k in range(count)
    ]
    in_specs += [pl.BlockSpec((TILE, width), lambda i, ix: (i, 0))] * count
    return pl.pallas_call(
        functools.partial(grad_kernel, count),
        out_shape=jax.ShapeDtypeStruct((rows, units), jnp.float32),
        grid_spec=pltpu.PrefetchScalarGridSpec(
            num_scalar_prefetch=1,
            grid=(units // TILE,),
            in_specs=in_specs,
            out_specs=pl.BlockSpec((rows, TILE), lambda i, ix: (0, i)),
        ),
        compiler_params=pltpu.CompilerParams(dimension_semantics=("arbitrary",)),
        cost_estimate=pl.CostEstimate(
            flops=2 * rows * units * count * width,
            bytes_accessed=units * count * width * 2 + rows * count * width * 2 + rows * units * 4,
            transcendentals=0,
        ),
    )(idx, *([cot] * count), *weights)


def split(x):
    high = x.astype(jnp.bfloat16)
    return high, (x - high.astype(jnp.float32)).astype(jnp.bfloat16)


def features_kernel(scale, idx, both, pick_left, pick_right, high_side, low_side, left_out, right_out, scores):
    f32 = jnp.float32

    def part(offset, width, pick):
        at = pl.multiple_of(offset, 128)
        high, low = split(jnp.concatenate([both[i, :, pl.ds(at, width)] for i in range(both.shape[0])], axis=0))
        return jnp.dot(pick, high, preferred_element_type=f32) + jnp.dot(pick, low, preferred_element_type=f32)

    def against(x, side):
        return lax.dot_general(x, side, (((1,), (1,)), ((), ())), preferred_element_type=f32)

    high, low = split(part(idx[0], left_out.shape[1], pick_left[...]))
    left_out[...] = jnp.concatenate([high, low, high], axis=0)
    high, low = split(part(idx[1], right_out.shape[1], pick_right[...]))
    right_out[...] = jnp.concatenate([high, high, low], axis=0)
    product = against(high, high_side[...]) + (against(low, high_side[...]) + against(high, low_side[...]))
    scores[...] = product * scale


def gram_kernel(scale, gram, left, right, *refs):
    out = refs[-1]
    term = lax.dot_general(
        left[...], right[...], (((0,), (0,)), ((), ())), preferred_element_type=jnp.float32
    )
    out[...] = gram[...] + term * scale


def local(
    n,
    m,
    inputs,
    cotangent,
    gate_pre,
    up_pre,
    down_weight,
    proj_model,
    proj_hidden,
    lengths,
    gram,
    inverse_factor,
    queries,
):
    top = lax.Precision.HIGHEST
    f32 = jnp.float32
    f = lax.axis_index("fsdp")
    s = lax.axis_index("solve")
    rows = inputs.shape[0]
    local_seqs = lengths.shape[0]
    half = proj_model.shape[1] // 2
    h = n // 2
    chips = n // 2
    side = f // h

    def swap(x, axis, size, bit):
        return lax.ppermute(x, axis, [(i, i ^ bit) for i in range(size)])

    def total(x, axis, size, bit=1):
        while bit < size:
            if 2 * bit < size:
                one, two, both = (swap(x, axis, size, b) for b in (bit, 2 * bit, 3 * bit))
                x = (x + one) + (two + both)
            else:
                x = x + swap(x, axis, size, bit)
            bit *= 4
        return x

    mirror_of = [(chips - 1 - i // 2) * 2 + i % 2 for i in range(n)]

    def mirror(x, keep=lambda chip: True):
        pairs = [(i, mirror_of[i]) for i in range(n) if keep(i // 2)]
        return lax.ppermute(x, "fsdp", pairs)

    def inner(chip):
        return chips // 4 <= chip < chips - chips // 4

    tiles = gate_pre.shape[1] // TILE
    blocks = {0: down_weight}
    step = 2
    while step < h:
        blocks.update({k ^ step: swap(v, "fsdp", n, step) for k, v in list(blocks.items())})
        step *= 2
    gate_inner = mirror(gate_pre, inner)
    cot_full = lax.all_gather(cotangent, "solve", axis=1, tiled=True)
    part = rows // m
    near = cot_full.shape[1] // 2
    quarter = lax.dynamic_slice(cot_full, (s * part, (1 - side) * near), (part, near))
    quarter = mirror(quarter)
    cot_far = lax.all_gather(quarter, "solve", axis=0, tiled=True)
    sibling = swap(down_weight, "fsdp", n, 1)
    blocks.update({k ^ 1: swap(v, "fsdp", n, 1) for k, v in list(blocks.items()) if k})
    blocks[1] = sibling
    order = sorted(blocks)
    weights = [blocks[k] for k in order]
    share = max(1, tiles // 7)
    cuts = [0, tiles - 3 * share, tiles - share, tiles]
    chunks = []
    for j, (a, b) in enumerate(zip(cuts[:-1], cuts[1:])):
        gate_outer, _ = lax.optimization_barrier((gate_pre[:, a * TILE : b * TILE], quarter))
        gate_outer = mirror(gate_outer, lambda chip: not inner(chip))
        chunks.append((j, a, b, gate_outer))

    gate = gate_pre.astype(f32)
    hidden = (gate * jax.nn.sigmoid(gate) * up_pre.astype(f32)).astype(jnp.bfloat16)
    early = jnp.concatenate(
        [
            jnp.dot(hidden, proj_hidden[:, :half], preferred_element_type=f32),
            jnp.dot(cotangent, proj_model[:, :half], preferred_element_type=f32),
            jnp.dot(inputs, proj_model[:, half:], preferred_element_type=f32),
        ],
        axis=1,
    )
    early = total(early, "solve", m)

    query_block = lax.all_gather(queries.astype(jnp.bfloat16), "fsdp", axis=1, tiled=True)
    partial = jnp.dot(inverse_factor, query_block.astype(f32), precision=lax.Precision.HIGH)
    whitened = partial
    bit = m // 2
    while bit:
        size = whitened.shape[0] // 2
        mine = s // bit % 2
        moved = swap(lax.dynamic_slice_in_dim(whitened, (1 - mine) * size, size, 0), "solve", m, bit)
        whitened = lax.dynamic_slice_in_dim(whitened, mine * size, size, 0) + moved
        bit //= 2
    whitened_rows = whitened
    bit = 1
    while bit < m:
        mine = s // bit % 2
        moved = swap(whitened_rows, "solve", m, bit)
        whitened_rows = jnp.where(
            mine == 0,
            jnp.concatenate([whitened_rows, moved], axis=0),
            jnp.concatenate([moved, whitened_rows], axis=0),
        )
        bit *= 2
    whitened_rows = lax.optimization_barrier(whitened_rows)
    query_side = lax.dot_general(whitened_rows, inverse_factor, (((0,), (0,)), ((), ())), precision=lax.Precision.HIGH)

    own_idx = jnp.stack([f ^ k for k in order]).astype(jnp.int32)
    far_idx = own_idx - side * h
    other_side = swap(query_side, "fsdp", n, 1)
    own_idx, query_side, _ = lax.optimization_barrier((own_idx, query_side, quarter))
    own = tokens(
        own_idx, cot_full, [(v, 0) for v in weights], [(gate_pre, 0)], None, proj_hidden, 0, tiles
    )
    token_index = lax.broadcasted_iota(jnp.int32, (rows, 1), 0)
    slots = lax.broadcasted_iota(jnp.int32, (1, local_seqs), 1)
    length_of = jnp.sum(
        jnp.where(token_index // SEQ_LEN == slots, lengths[None, :], 0), axis=1, keepdims=True
    )
    weight_of = jnp.where(
        token_index % SEQ_LEN < length_of, 1.0 / jnp.sqrt(length_of.astype(f32)), 0.0
    )
    in_down = early[:, :half]
    out_down = early[:, half : 2 * half] * weight_of
    in_up = early[:, 2 * half :] * weight_of
    in_up_far = mirror(lax.dynamic_slice_in_dim(in_up.astype(jnp.bfloat16), s * part, part, 0))

    def pair(outs, ins):
        shape = (local_seqs, SEQ_LEN, half)
        feat = jnp.einsum("eto,eti->eoi", outs.reshape(shape), ins.reshape(shape), precision=top)
        return feat.reshape(local_seqs, half * half)

    down = pair(out_down, in_down)
    up_own = total(pair(own[:, half:], in_up), "solve", m)

    own, in_up_far = lax.optimization_barrier((own, in_up_far))
    in_up_far = lax.all_gather(in_up_far, "solve", axis=0, tiled=True)
    grad = gradient(far_idx, cot_far, weights)
    far = None
    for j, a, b, gate_outer in chunks:
        if far is not None:
            gate_outer, far = lax.optimization_barrier((gate_outer, far))
        units = slice(a * TILE, b * TILE)
        gate = gate_inner[:, units].astype(f32) + gate_outer.astype(f32)
        grad_up = (grad[:, units] * (gate * jax.nn.sigmoid(gate))).astype(jnp.bfloat16)
        term = jnp.dot(grad_up, proj_hidden[units, half:], preferred_element_type=f32)
        far = term if far is None else far + term
    up_far = pair(far, in_up_far.astype(f32))
    query_side = query_side + other_side
    high = lax.reduce_precision(query_side, 8, 7)
    query_side = (high.astype(jnp.bfloat16), (query_side - high).astype(jnp.bfloat16))
    moved = [
        lax.ppermute(
            up_far,
            ("fsdp", "solve"),
            [(i * m + j, mirror_of[i] * m + (j ^ k)) for i in range(n) for j in range(m)],
        )
        for k in range(min(m, 4))
    ]
    while len(moved) > 1:
        moved = [one + two for one, two in zip(moved[::2], moved[1::2])]
    up = up_own + total(moved[0], "solve", m, 4)
    both = lax.all_gather(jnp.concatenate([up, down], axis=0), "fsdp", axis=0)

    examples = n * local_seqs
    row_width = gram.shape[0]
    col_width = gram.shape[1]
    count = queries.shape[1] * n
    size = half * half

    def place(offset):
        up_part = offset >= size
        shape = (examples, 2 * examples)
        row = lax.broadcasted_iota(jnp.int32, shape, 0)
        column = lax.broadcasted_iota(jnp.int32, shape, 1)
        wanted = row // local_seqs * 2 * local_seqs + row % local_seqs + jnp.where(up_part, 0, local_seqs)
        return (column == wanted).astype(jnp.bfloat16), jnp.where(up_part, offset - size, offset)

    pick_left, at_left = place(f * row_width)
    pick_right, at_right = place(s * col_width)
    at = jnp.stack([at_left, at_right]).astype(jnp.int32)
    left, right, scores = pl.pallas_call(
        functools.partial(features_kernel, 1.0 / math.sqrt(2 * size)),
        out_shape=(
            jax.ShapeDtypeStruct((3 * examples, row_width), jnp.bfloat16),
            jax.ShapeDtypeStruct((3 * examples, col_width), jnp.bfloat16),
            jax.ShapeDtypeStruct((examples, count), f32),
        ),
        in_specs=[pl.BlockSpec(memory_space=pltpu.SMEM)] + [pl.BlockSpec(memory_space=pltpu.VMEM)] * 5,
    )(at, both, pick_left, pick_right, *query_side)
    scores = total(scores, "fsdp", n, 2)
    scores = total(scores, "solve", m)
    block = 128
    steps = row_width // block
    ends = [0, steps // 2, steps]
    new_gram = None
    for a, b in zip(ends[:-1], ends[1:]):
        in_specs = [
            pl.BlockSpec((block, col_width), functools.partial(lambda z, i: (z + i, 0), a)),
            pl.BlockSpec((3 * examples, block), functools.partial(lambda z, i: (0, z + i), a)),
            pl.BlockSpec((3 * examples, col_width), lambda i: (0, 0)),
        ]
        operands = [gram, left, right]
        if new_gram is not None:
            in_specs.append(pl.BlockSpec(memory_space=pl.ANY))
            operands.append(new_gram)
        new_gram = pl.pallas_call(
            functools.partial(gram_kernel, 1.0 / examples),
            out_shape=jax.ShapeDtypeStruct(gram.shape, f32),
            grid=(b - a,),
            in_specs=in_specs,
            out_specs=pl.BlockSpec((block, col_width), functools.partial(lambda z, i: (z + i, 0), a)),
            input_output_aliases={} if new_gram is None else {3: 0},
        )(*operands)
    return (new_gram, whitened, scores)


def solution(mesh):
    in_specs = (
        P("fsdp", "solve"),
        P("fsdp", "solve"),
        P("fsdp", "solve"),
        P("fsdp", "solve"),
        P("solve", "fsdp"),
        P("solve", None),
        P("solve", None),
        P("fsdp"),
        P("fsdp", "solve"),
        P("fsdp", "solve"),
        P("solve", "fsdp"),
    )
    out_specs = (P("fsdp", "solve"), P(("fsdp", "solve"), None), P())

    def body(*args):
        return local(mesh.shape["fsdp"], mesh.shape["solve"], *args)

    return jax.shard_map(body, mesh=mesh, in_specs=in_specs, out_specs=out_specs, check_vma=False)
```

```python
import functools
import math

import jax
import jax.numpy as jnp
from jax import lax
from jax.experimental import pallas as pl
from jax.experimental.pallas import tpu as pltpu
from jax.sharding import PartitionSpec as P


SEQ_LEN = 256
TILE = 256


def tokens_kernel(count, gates, chained, idx, *refs):
    del idx
    cots, refs = refs[:count], refs[count:]
    weights, refs = refs[:count], refs[count:]
    gate_refs, refs = refs[:gates], refs[gates:]
    if chained:
        start, refs = refs[0], refs[1:]
    proj, out = refs

    @pl.when(pl.program_id(0) == 0)
    def _():
        out[...] = start[...] if chained else jnp.zeros_like(out)

    grad = None
    for cot, weight in zip(cots, weights):
        term = lax.dot_general(
            cot[...], weight[...], (((1,), (1,)), ((), ())), preferred_element_type=jnp.float32
        )
        grad = term if grad is None else grad + term
    gate = gate_refs[0][...].astype(jnp.float32)
    for other in gate_refs[1:]:
        gate = gate + other[...].astype(jnp.float32)
    smooth = gate * jax.nn.sigmoid(gate)
    grad_up = (grad * smooth).astype(jnp.bfloat16)
    out[...] += jnp.dot(grad_up, proj[...], preferred_element_type=jnp.float32)


def tokens(idx, cot, weights, gate_parts, start, proj, first, tiles):
    count = len(weights)
    rows = cot.shape[0]
    width = weights[0][0].shape[1]
    in_specs = [
        pl.BlockSpec(
            (rows, width), functools.partial(lambda k, i, ix: (0, ix[k]), k), pipeline_mode=pl.Buffered(1)
        )
        for k in range(count)
    ]
    for _, shift in weights:
        in_specs.append(pl.BlockSpec((TILE, width), functools.partial(lambda a, i, ix: (a + i, 0), shift)))
    for _, shift in gate_parts:
        in_specs.append(pl.BlockSpec((rows, TILE), functools.partial(lambda a, i, ix: (0, a + i), shift)))
    operands = [cot] * count + [part for part, _ in weights] + [part for part, _ in gate_parts]
    whole = pl.BlockSpec((rows, proj.shape[1]), lambda i, ix: (0, 0))
    if start is not None:
        in_specs.append(whole)
        operands.append(start)
    in_specs.append(pl.BlockSpec((TILE, proj.shape[1]), lambda i, ix: (first + i, 0)))
    operands.append(proj)
    return pl.pallas_call(
        functools.partial(tokens_kernel, count, len(gate_parts), start is not None),
        out_shape=jax.ShapeDtypeStruct((rows, proj.shape[1]), jnp.float32),
        grid_spec=pltpu.PrefetchScalarGridSpec(
            num_scalar_prefetch=1,
            grid=(tiles,),
            in_specs=in_specs,
            out_specs=whole,
        ),
        compiler_params=pltpu.CompilerParams(dimension_semantics=("arbitrary",)),
        cost_estimate=pl.CostEstimate(
            flops=2 * rows * TILE * tiles * (count * width + 256),
            bytes_accessed=TILE * tiles * (count * width + 2 * rows) * 2 + rows * count * width * 2,
            transcendentals=rows * TILE * tiles,
        ),
    )(idx, *operands)


def grad_kernel(count, idx, *refs):
    del idx
    out = refs[-1]
    grad = None
    for cot, weight in zip(refs[:count], refs[count : 2 * count]):
        term = lax.dot_general(
            cot[...], weight[...], (((1,), (1,)), ((), ())), preferred_element_type=jnp.float32
        )
        grad = term if grad is None else grad + term
    out[...] = grad


def gradient(idx, cot, weights):
    count = len(weights)
    rows = cot.shape[0]
    units, width = weights[0].shape
    in_specs = [
        pl.BlockSpec(
            (rows, width), functools.partial(lambda k, i, ix: (0, ix[k]), k), pipeline_mode=pl.Buffered(1)
        )
        for k in range(count)
    ]
    in_specs += [pl.BlockSpec((TILE, width), lambda i, ix: (i, 0))] * count
    return pl.pallas_call(
        functools.partial(grad_kernel, count),
        out_shape=jax.ShapeDtypeStruct((rows, units), jnp.float32),
        grid_spec=pltpu.PrefetchScalarGridSpec(
            num_scalar_prefetch=1,
            grid=(units // TILE,),
            in_specs=in_specs,
            out_specs=pl.BlockSpec((rows, TILE), lambda i, ix: (0, i)),
        ),
        compiler_params=pltpu.CompilerParams(dimension_semantics=("arbitrary",)),
        cost_estimate=pl.CostEstimate(
            flops=2 * rows * units * count * width,
            bytes_accessed=units * count * width * 2 + rows * count * width * 2 + rows * units * 4,
            transcendentals=0,
        ),
    )(idx, *([cot] * count), *weights)


def split(x):
    high = x.astype(jnp.bfloat16)
    return high, (x - high.astype(jnp.float32)).astype(jnp.bfloat16)


def features_kernel(scale, idx, both, pick_left, pick_right, high_side, low_side, left_out, right_out, scores):
    f32 = jnp.float32

    def part(offset, width, pick):
        at = pl.multiple_of(offset, 128)
        high, low = split(jnp.concatenate([both[i, :, pl.ds(at, width)] for i in range(both.shape[0])], axis=0))
        return jnp.dot(pick, high, preferred_element_type=f32) + jnp.dot(pick, low, preferred_element_type=f32)

    def against(x, side):
        return lax.dot_general(x, side, (((1,), (1,)), ((), ())), preferred_element_type=f32)

    high, low = split(part(idx[0], left_out.shape[1], pick_left[...]))
    left_out[...] = jnp.concatenate([high, low, high], axis=0)
    high, low = split(part(idx[1], right_out.shape[1], pick_right[...]))
    right_out[...] = jnp.concatenate([high, high, low], axis=0)
    product = against(high, high_side[...]) + (against(low, high_side[...]) + against(high, low_side[...]))
    scores[...] = product * scale


def gram_kernel(scale, gram, left, right, *refs):
    out = refs[-1]
    term = lax.dot_general(
        left[...], right[...], (((0,), (0,)), ((), ())), preferred_element_type=jnp.float32
    )
    out[...] = gram[...] + term * scale


def local(
    n,
    m,
    inputs,
    cotangent,
    gate_pre,
    up_pre,
    down_weight,
    proj_model,
    proj_hidden,
    lengths,
    gram,
    inverse_factor,
    queries,
):
    top = lax.Precision.HIGHEST
    f32 = jnp.float32
    f = lax.axis_index("fsdp")
    s = lax.axis_index("solve")
    rows = inputs.shape[0]
    local_seqs = lengths.shape[0]
    half = proj_model.shape[1] // 2
    h = n // 2
    chips = n // 2
    side = f // h

    def swap(x, axis, size, bit):
        return lax.ppermute(x, axis, [(i, i ^ bit) for i in range(size)])

    def total(x, axis, size, bit=1):
        while bit < size:
            if 2 * bit < size:
                one, two, both = (swap(x, axis, size, b) for b in (bit, 2 * bit, 3 * bit))
                x = (x + one) + (two + both)
            else:
                x = x + swap(x, axis, size, bit)
            bit *= 4
        return x

    mirror_of = [(chips - 1 - i // 2) * 2 + i % 2 for i in range(n)]

    def mirror(x, keep=lambda chip: True):
        pairs = [(i, mirror_of[i]) for i in range(n) if keep(i // 2)]
        return lax.ppermute(x, "fsdp", pairs)

    def inner(chip):
        return chips // 4 <= chip < chips - chips // 4

    tiles = gate_pre.shape[1] // TILE
    blocks = {0: down_weight}
    step = 2
    while step < h:
        blocks.update({k ^ step: swap(v, "fsdp", n, step) for k, v in list(blocks.items())})
        step *= 2
    gate_inner = mirror(gate_pre, inner)
    cot_full = lax.all_gather(cotangent, "solve", axis=1, tiled=True)
    part = rows // m
    near = cot_full.shape[1] // 2
    quarter = lax.dynamic_slice(cot_full, (s * part, (1 - side) * near), (part, near))
    quarter = mirror(quarter)
    cot_far = lax.all_gather(quarter, "solve", axis=0, tiled=True)
    sibling = swap(down_weight, "fsdp", n, 1)
    blocks.update({k ^ 1: swap(v, "fsdp", n, 1) for k, v in list(blocks.items()) if k})
    blocks[1] = sibling
    order = sorted(blocks)
    weights = [blocks[k] for k in order]
    share = max(1, tiles // 7)
    cuts = [0, tiles - 3 * share, tiles - share, tiles]
    chunks = []
    for j, (a, b) in enumerate(zip(cuts[:-1], cuts[1:])):
        gate_outer, _ = lax.optimization_barrier((gate_pre[:, a * TILE : b * TILE], quarter))
        gate_outer = mirror(gate_outer, lambda chip: not inner(chip))
        chunks.append((j, a, b, gate_outer))

    gate = gate_pre.astype(f32)
    hidden = (gate * jax.nn.sigmoid(gate) * up_pre.astype(f32)).astype(jnp.bfloat16)
    early = jnp.concatenate(
        [
            jnp.dot(hidden, proj_hidden[:, :half], preferred_element_type=f32),
            jnp.dot(cotangent, proj_model[:, :half], preferred_element_type=f32),
            jnp.dot(inputs, proj_model[:, half:], preferred_element_type=f32),
        ],
        axis=1,
    )
    early = total(early, "solve", m)

    query_block = lax.all_gather(queries.astype(jnp.bfloat16), "fsdp", axis=1, tiled=True)
    partial = jnp.dot(inverse_factor, query_block.astype(f32), precision=lax.Precision.HIGH)
    whitened = partial
    bit = m // 2
    while bit:
        size = whitened.shape[0] // 2
        mine = s // bit % 2
        moved = swap(lax.dynamic_slice_in_dim(whitened, (1 - mine) * size, size, 0), "solve", m, bit)
        whitened = lax.dynamic_slice_in_dim(whitened, mine * size, size, 0) + moved
        bit //= 2
    whitened_rows = whitened
    bit = 1
    while bit < m:
        mine = s // bit % 2
        moved = swap(whitened_rows, "solve", m, bit)
        whitened_rows = jnp.where(
            mine == 0,
            jnp.concatenate([whitened_rows, moved], axis=0),
            jnp.concatenate([moved, whitened_rows], axis=0),
        )
        bit *= 2
    whitened_rows = lax.optimization_barrier(whitened_rows)
    query_side = lax.dot_general(whitened_rows, inverse_factor, (((0,), (0,)), ((), ())), precision=lax.Precision.HIGH)

    own_idx = jnp.stack([f ^ k for k in order]).astype(jnp.int32)
    far_idx = own_idx - side * h
    other_side = swap(query_side, "fsdp", n, 1)
    own_idx, query_side, _ = lax.optimization_barrier((own_idx, query_side, quarter))
    own = tokens(
        own_idx, cot_full, [(v, 0) for v in weights], [(gate_pre, 0)], None, proj_hidden, 0, tiles
    )
    token_index = lax.broadcasted_iota(jnp.int32, (rows, 1), 0)
    slots = lax.broadcasted_iota(jnp.int32, (1, local_seqs), 1)
    length_of = jnp.sum(
        jnp.where(token_index // SEQ_LEN == slots, lengths[None, :], 0), axis=1, keepdims=True
    )
    weight_of = jnp.where(
        token_index % SEQ_LEN < length_of, 1.0 / jnp.sqrt(length_of.astype(f32)), 0.0
    )
    in_down = early[:, :half]
    out_down = early[:, half : 2 * half] * weight_of
    in_up = early[:, 2 * half :] * weight_of
    in_up_far = mirror(lax.dynamic_slice_in_dim(in_up.astype(jnp.bfloat16), s * part, part, 0))

    def pair(outs, ins):
        shape = (local_seqs, SEQ_LEN, half)
        feat = jnp.einsum("eto,eti->eoi", outs.reshape(shape), ins.reshape(shape), precision=top)
        return feat.reshape(local_seqs, half * half)

    down = pair(out_down, in_down)
    up_own = pair(own[:, half:], in_up)

    own, in_up_far = lax.optimization_barrier((own, in_up_far))
    in_up_far = lax.all_gather(in_up_far, "solve", axis=0, tiled=True)
    grad = gradient(far_idx, cot_far, weights)
    far = None
    for j, a, b, gate_outer in chunks:
        if far is not None:
            gate_outer, far = lax.optimization_barrier((gate_outer, far))
        units = slice(a * TILE, b * TILE)
        gate = gate_inner[:, units].astype(f32) + gate_outer.astype(f32)
        grad_up = (grad[:, units] * (gate * jax.nn.sigmoid(gate))).astype(jnp.bfloat16)
        term = jnp.dot(grad_up, proj_hidden[units, half:], preferred_element_type=f32)
        far = term if far is None else far + term
    up_far = pair(far, in_up_far.astype(f32))
    query_side = query_side + other_side
    high = lax.reduce_precision(query_side, 8, 7)
    query_side = (high.astype(jnp.bfloat16), (query_side - high).astype(jnp.bfloat16))
    up = up_own + mirror(up_far)
    up = total(up, "solve", m)
    both = lax.all_gather(jnp.concatenate([up, down], axis=0), "fsdp", axis=0)

    examples = n * local_seqs
    row_width = gram.shape[0]
    col_width = gram.shape[1]
    count = queries.shape[1] * n
    size = half * half

    def place(offset):
        up_part = offset >= size
        shape = (examples, 2 * examples)
        row = lax.broadcasted_iota(jnp.int32, shape, 0)
        column = lax.broadcasted_iota(jnp.int32, shape, 1)
        wanted = row // local_seqs * 2 * local_seqs + row % local_seqs + jnp.where(up_part, 0, local_seqs)
        return (column == wanted).astype(jnp.bfloat16), jnp.where(up_part, offset - size, offset)

    pick_left, at_left = place(f * row_width)
    pick_right, at_right = place(s * col_width)
    at = jnp.stack([at_left, at_right]).astype(jnp.int32)
    left, right, scores = pl.pallas_call(
        functools.partial(features_kernel, 1.0 / math.sqrt(2 * size)),
        out_shape=(
            jax.ShapeDtypeStruct((3 * examples, row_width), jnp.bfloat16),
            jax.ShapeDtypeStruct((3 * examples, col_width), jnp.bfloat16),
            jax.ShapeDtypeStruct((examples, count), f32),
        ),
        in_specs=[pl.BlockSpec(memory_space=pltpu.SMEM)] + [pl.BlockSpec(memory_space=pltpu.VMEM)] * 5,
    )(at, both, pick_left, pick_right, *query_side)
    scores = total(scores, "fsdp", n, 2)
    scores = total(scores, "solve", m)
    block = 256
    steps = row_width // block
    ends = [0, steps // 2, steps]
    new_gram = None
    for a, b in zip(ends[:-1], ends[1:]):
        in_specs = [
            pl.BlockSpec((block, col_width), functools.partial(lambda z, i: (z + i, 0), a)),
            pl.BlockSpec((3 * examples, block), functools.partial(lambda z, i: (0, z + i), a)),
            pl.BlockSpec((3 * examples, col_width), lambda i: (0, 0)),
        ]
        operands = [gram, left, right]
        if new_gram is not None:
            in_specs.append(pl.BlockSpec(memory_space=pl.ANY))
            operands.append(new_gram)
        new_gram = pl.pallas_call(
            functools.partial(gram_kernel, 1.0 / examples),
            out_shape=jax.ShapeDtypeStruct(gram.shape, f32),
            grid=(b - a,),
            in_specs=in_specs,
            out_specs=pl.BlockSpec((block, col_width), functools.partial(lambda z, i: (z + i, 0), a)),
            input_output_aliases={} if new_gram is None else {3: 0},
        )(*operands)
    return (new_gram, whitened, scores)


def solution(mesh):
    in_specs = (
        P("fsdp", "solve"),
        P("fsdp", "solve"),
        P("fsdp", "solve"),
        P("fsdp", "solve"),
        P("solve", "fsdp"),
        P("solve", None),
        P("solve", None),
        P("fsdp"),
        P("fsdp", "solve"),
        P("fsdp", "solve"),
        P("solve", "fsdp"),
    )
    out_specs = (P("fsdp", "solve"), P(("fsdp", "solve"), None), P())

    def body(*args):
        return local(mesh.shape["fsdp"], mesh.shape["solve"], *args)

    return jax.shard_map(body, mesh=mesh, in_specs=in_specs, out_specs=out_specs, check_vma=False)
```
